256 devices in a mesh: pipe: 4 (over x), seq: 16 (over z, core), chan: 4 (over y).
Axes of the slice: x: 4, y: 4, z: 8, core: 2. Of those that a mesh axis runs over, the one named last changes fastest.
Arguments:
- signal: bfloat16 [4, 4096, 2048], P('pipe', 'seq', 'chan'), may hold values from -6 to 6
- gate_value: bfloat16 [4, 4096, 2048], P('pipe', 'seq', 'chan'), may hold values from -6 to 6
- grad_out: bfloat16 [4, 4096, 2048], P('pipe', 'seq', 'chan'), may hold values from -1.5 to 1.5
- long_filter: bfloat16 [4, 4096, 2048], P('pipe', 'seq', 'chan'), may hold values from -0.09375 to 0.09375
- weight: bfloat16 [4, 4096, 2048], P('pipe', None, 'chan'), may hold values from -0.125 to 0.125
Outputs:
- gate_grad: bfloat16 [4, 4096, 2048], P('pipe', 'seq', 'chan')
- filter_grad: float32 [4, 4096, 2048], P('pipe', 'seq', 'chan')
- input_grad: bfloat16 [4, 4096, 4096], P('pipe', 'seq', 'chan')
The draws below stay inside these ranges and needn't reach their ends.
All inputs are finite; a program needn't handle non-finite values.
Results may differ from the reference program's by a relative error of at most 0.02.
Values may be sent and summed in bfloat16 or wider, within the bound.
No kernel may reach another device: no remote copies, remote signals or barrier semaphores. Data moves between devices by JAX's collectives and lax.ppermute only.
A program may use at most 128 MiB of HBM per device.

```python
import jax
import jax.numpy as jnp
from jax import lax

D = 4096
CH = 2048
SECTIONS = 4
SEQ_LEN = 4096


def block_levels(rng, dims, pieces, low, top_value):
    loudness, own = 1.0, jax.random.fold_in(rng, 6)
    for dim, blocks in pieces:
        draws = jnp.exp(jax.random.uniform(jax.random.fold_in(own, dim), (blocks,), jnp.float32, low / len(pieces), top_value / len(pieces)))
        loudness = loudness * jnp.repeat(draws, dims[dim] // blocks).reshape([-1 if axis == dim else 1 for axis in range(len(dims))])
    return loudness


def normal_values(stream_key, dims, deviation, reach, cuts=(), dtype=jnp.bfloat16):
    factor_of = block_levels(stream_key, dims, cuts, -0.22, 0.18) if cuts else 1.0
    drawn = jax.random.normal(stream_key, dims, jnp.float32) * deviation * factor_of
    return jnp.minimum(jnp.maximum(drawn, -reach), reach).astype(dtype)


def setup_inputs(seed: int = 0) -> dict:
    key_list = jax.random.split(jax.random.key(seed), 6)
    signal = normal_values(key_list[0], (SECTIONS, SEQ_LEN, CH), 1.0, 6.0, ((0, 4), (1, 16), (2, 4)))
    gate_value = normal_values(key_list[1], (SECTIONS, SEQ_LEN, CH), 1.0, 6.0, ((0, 4), (1, 16), (2, 4)))
    grad_out = normal_values(key_list[2], (SECTIONS, SEQ_LEN, CH), 0.25, 1.5, ((0, 4), (1, 16), (2, 4)))
    long_filter = normal_values(key_list[3], (SECTIONS, SEQ_LEN, CH), SEQ_LEN ** -0.5, 0.09375, ((0, 4), (1, 16), (2, 4)))
    weight = normal_values(key_list[4], (SECTIONS, D, CH), CH ** -0.5, 0.125, ((0, 4), (2, 4)))
    return dict(signal=signal, gate_value=gate_value, grad_out=grad_out, long_filter=long_filter, weight=weight)


def causal(left_side, right_side):
    seq_length = left_side.shape[0]
    product = jnp.fft.rfft(left_side, 2 * seq_length, axis=0) * jnp.fft.rfft(right_side, 2 * seq_length, axis=0)
    return jnp.fft.irfft(product, 2 * seq_length, axis=0)[:seq_length]


def filter_section(section_items):
    signal, gate_value, grad_out, long_filter = section_items
    signal = signal.astype(jnp.float32)
    grad_wide = grad_out.astype(jnp.float32)
    filter_wide = long_filter.astype(jnp.float32)
    gated_low = (gate_value.astype(jnp.float32) * grad_wide).astype(jnp.bfloat16)
    gated = lax.optimization_barrier(gated_low).astype(jnp.float32)
    conv = causal(filter_wide, signal)
    gate_grad = (grad_wide * conv).astype(jnp.bfloat16)
    signal_grad = causal(filter_wide, gated[::-1])[::-1].astype(jnp.bfloat16)
    filter_grad = causal(signal, gated[::-1])[::-1].astype(jnp.float32)
    return gate_grad, filter_grad, signal_grad


def project_section(section_items):
    received, weight = section_items
    return jnp.dot(received, weight.T, preferred_element_type=jnp.float32).astype(jnp.bfloat16)


def reference(signal, gate_value, grad_out, long_filter, weight):
    gate_grad, filter_grad, signal_grad = lax.map(filter_section, (signal, gate_value, grad_out, long_filter))
    received = jnp.roll(signal_grad, -1, axis=0)
    input_grad = lax.map(project_section, (received, weight))
    return gate_grad, filter_grad, input_grad
```

```python
import jax
import jax.numpy as jnp
import ml_dtypes
import numpy as np
from jax import lax
from jax.experimental import pallas as pl
from jax.experimental.pallas import tpu as pltpu
from jax.sharding import PartitionSpec as P


def make_tables(panel_len):
    position = np.arange(panel_len)[:, None]
    odd = 2 * np.arange(panel_len)[None, :] + 1
    angles = (position * odd % (4 * panel_len)) * (np.pi / (2 * panel_len))
    table = np.concatenate([np.cos(angles), -np.sin(angles)], axis=1)
    high = table.astype(np.float32).astype(ml_dtypes.bfloat16)
    low = (table - high.astype(np.float64)).astype(np.float32).astype(ml_dtypes.bfloat16)
    return high, low


def dot(left, right):
    return jnp.dot(left, right, preferred_element_type=jnp.float32)


def spectra(rows_ref, high_ref, low_ref):
    rows = rows_ref[...]
    return dot(rows, high_ref[...]) + dot(rows, low_ref[...])


def inverse(spec, high_ref, low_ref):
    panel_len = high_ref.shape[0]
    top = spec.astype(jnp.bfloat16)
    rest = (spec - top.astype(jnp.float32)).astype(jnp.bfloat16)
    dims = (((1,), (1,)), ((), ()))

    def back(left, right):
        return lax.dot_general(left, right, dims, preferred_element_type=jnp.float32)

    high = high_ref[...]
    return (back(top, high) + (back(rest, high) + back(top, low_ref[...]))) * (1.0 / panel_len)


def widen(plain_ref, full_ref, chans, panels):
    half = plain_ref.shape[1] // 2
    sign = 1.0 - 2.0 * (lax.broadcasted_iota(jnp.int32, (chans, half), 1) % 2).astype(jnp.float32)
    full_ref[pl.ds(0, chans), :] = plain_ref[pl.ds(0, chans), :]
    for panel in range(1, panels):
        now, prior = pl.ds(panel * chans, chans), pl.ds((panel - 1) * chans, chans)
        full_ref[now, :half] = plain_ref[now, :half] - sign * plain_ref[prior, half:]
        full_ref[now, half:] = plain_ref[now, half:] + sign * plain_ref[prior, :half]


def pair_sums(out_ref, one_ref, lag_ref, chans, panels, forward):
    half = out_ref.shape[1] // 2
    group = 4
    for lane in range(0, half, 128):

        def step(row, carry):
            start = pl.multiple_of(row * 8, 8)

            def load(ref, panel):
                rows = pl.ds(panel * chans + start, 8)
                return ref[rows, lane : lane + 128], ref[rows, half + lane : half + lane + 128]

            for first in range(0, panels, group):
                sums = [None] * group
                ones = {}
                lags = range(first + group) if forward else range(panels - first)
                for lag in lags:
                    lag_re, lag_im = load(lag_ref, lag)
                    for at in range(group):
                        other = first + at - lag if forward else first + at + lag
                        if not 0 <= other < panels:
                            continue
                        if other not in ones:
                            ones[other] = load(one_ref, other)
                        one_re, one_im = ones[other]
                        if forward:
                            re = one_re * lag_re - one_im * lag_im
                            im = one_re * lag_im + one_im * lag_re
                        else:
                            re = one_re * lag_re + one_im * lag_im
                            im = one_im * lag_re - one_re * lag_im
                        held = sums[at]
                        sums[at] = (re, im) if held is None else (held[0] + re, held[1] + im)
                for at in range(group):
                    rows = pl.ds((first + at) * chans + start, 8)
                    out_ref[rows, lane : lane + 128] = sums[at][0]
                    out_ref[rows, half + lane : half + lane + 128] = sums[at][1]
            return carry

        lax.fori_loop(0, chans // 8, step, 0)


def signal_grad_kernel(
    panels, gated_ref, filter_ref, high_ref, low_ref, grad_ref, gated_spec, filter_full, plain, sums
):
    chans = gated_ref.shape[0] // panels
    gated_spec[...] = spectra(gated_ref, high_ref, low_ref)
    plain[...] = spectra(filter_ref, high_ref, low_ref)
    widen(plain, filter_full, chans, panels)
    pair_sums(sums, gated_spec, filter_full, chans, panels, False)
    grad_ref[...] = inverse(sums[...], high_ref, low_ref).astype(grad_ref.dtype)


def rest_kernel(
    panels, signal_ref, gated_spec, filter_full, high_ref, low_ref, conv_ref, grad_ref, plain, full, sums
):
    chans = signal_ref.shape[0] // panels
    plain[...] = spectra(signal_ref, high_ref, low_ref)
    widen(plain, full, chans, panels)
    pair_sums(sums, plain, filter_full, chans, panels, True)
    conv_ref[...] = inverse(sums[...], high_ref, low_ref).astype(conv_ref.dtype)
    pair_sums(sums, gated_spec, full, chans, panels, False)
    grad_ref[...] = inverse(sums[...], high_ref, low_ref).astype(grad_ref.dtype)


def whole(count):
    return [pl.BlockSpec(memory_space=pltpu.VMEM)] * count


def call(kernel, panels, outs, scratch, *operands):
    return pl.pallas_call(
        lambda *refs: kernel(panels, *refs),
        out_shape=outs,
        in_specs=whole(len(operands)),
        out_specs=whole(len(outs)),
        scratch_shapes=scratch,
        compiler_params=pltpu.CompilerParams(vmem_limit_bytes=40 * 1024 * 1024),
    )(*operands)


def on_device(signal, gate_value, grad_out, long_filter, weight):
    panel_len, width = signal.shape[1:]
    panels = lax.axis_size("seq")
    groups = lax.axis_size("chan")
    chans = width // panels
    rows = panels * chans
    high, low = make_tables(panel_len)
    high, low = jnp.asarray(high), jnp.asarray(low)

    def to_channels(panel):
        parts = panel.T.reshape(panels, chans, panel_len)
        return lax.all_to_all(parts, "seq", 0, 0, tiled=True).reshape(rows, panel_len)

    def to_panels(by_channel):
        parts = by_channel.reshape(panels, chans, panel_len)
        return lax.all_to_all(parts, "seq", 0, 0, tiled=True).reshape(width, panel_len)

    weight_parts = weight[0].reshape(groups, weight.shape[1] // groups, width)
    weights = lax.all_to_all(weight_parts, "chan", 0, 0, tiled=True)

    gated = (gate_value[0].astype(jnp.float32) * grad_out[0].astype(jnp.float32)).astype(
        jnp.bfloat16
    )
    gated_rows = to_channels(gated)
    filter_rows = to_channels(long_filter[0])
    signal_rows = to_channels(signal[0])

    spec = jax.ShapeDtypeStruct((rows, 2 * panel_len), jnp.float32)
    back = jax.ShapeDtypeStruct((rows, panel_len), jnp.bfloat16)
    held = pltpu.VMEM((rows, 2 * panel_len), jnp.float32)
    signal_grad, gated_spec, filter_full = call(
        signal_grad_kernel, panels, (back, spec, spec), [held, held], gated_rows, filter_rows, high, low
    )
    conv, filter_grad = call(
        rest_kernel,
        panels,
        (back, back),
        [held, held, held],
        signal_rows,
        gated_spec,
        filter_full,
        high,
        low,
    )
    signal_grad = to_panels(signal_grad)
    sections = lax.axis_size("pipe")
    received = lax.ppermute(
        signal_grad, "pipe", [(i, (i - 1) % sections) for i in range(sections)]
    )
    copies = jnp.broadcast_to(received[None], (groups, width, panel_len))
    all_received = lax.all_to_all(copies, "chan", 0, 0, tiled=True)
    input_grad = lax.dot_general(
        all_received, weights, (((0, 1), (0, 2)), ((), ())), preferred_element_type=jnp.float32
    ).astype(jnp.bfloat16)
    conv = to_panels(conv).T
    gate_grad = (grad_out[0].astype(jnp.float32) * conv.astype(jnp.float32)).astype(jnp.bfloat16)
    filter_grad = to_panels(filter_grad).T.astype(jnp.float32)
    return gate_grad[None], filter_grad[None], input_grad[None]


def solution(mesh):
    return jax.shard_map(
        on_device,
        mesh=mesh,
        in_specs=(
            P("pipe", "seq", "chan"),
            P("pipe", "seq", "chan"),
            P("pipe", "seq", "chan"),
            P("pipe", "seq", "chan"),
            P("pipe", None, "chan"),
        ),
        out_specs=(P("pipe", "seq", "chan"), P("pipe", "seq", "chan"), P("pipe", "seq", "chan")),
        check_vma=False,
    )
```

```python
import jax
import jax.numpy as jnp
import ml_dtypes
import numpy as np
from jax import lax
from jax.experimental import pallas as pl
from jax.experimental.pallas import tpu as pltpu
from jax.sharding import PartitionSpec as P


def make_tables(panel_len):
    position = np.arange(panel_len)[:, None]
    odd = 2 * np.arange(panel_len)[None, :] + 1
    angles = (position * odd % (4 * panel_len)) * (np.pi / (2 * panel_len))
    table = np.concatenate([np.cos(angles), -np.sin(angles)], axis=1)
    high = table.astype(np.float32).astype(ml_dtypes.bfloat16)
    low = (table - high.astype(np.float64)).astype(np.float32).astype(ml_dtypes.bfloat16)
    return high, low


def dot(left, right):
    return jnp.dot(left, right, preferred_element_type=jnp.float32)


def spectra(rows, high_ref, low_ref):
    return dot(rows, high_ref[...]) + dot(rows, low_ref[...])


def inverse(spec, high_ref, low_ref):
    panel_len = high_ref.shape[0]
    top = spec.astype(jnp.bfloat16)
    rest = (spec - top.astype(jnp.float32)).astype(jnp.bfloat16)
    dims = (((1,), (1,)), ((), ()))

    def back(left, right):
        return lax.dot_general(left, right, dims, preferred_element_type=jnp.float32)

    high = high_ref[...]
    return (back(top, high) + (back(rest, high) + back(top, low_ref[...]))) * (1.0 / panel_len)


def widen(plain_ref, full_ref, chans, panels):
    half = plain_ref.shape[1] // 2
    sign = 1.0 - 2.0 * (lax.broadcasted_iota(jnp.int32, (chans, half), 1) % 2).astype(jnp.float32)
    full_ref[pl.ds(0, chans), :] = plain_ref[pl.ds(0, chans), :]
    for panel in range(1, panels):
        now, prior = pl.ds(panel * chans, chans), pl.ds((panel - 1) * chans, chans)
        full_ref[now, :half] = plain_ref[now, :half] - sign * plain_ref[prior, half:]
        full_ref[now, half:] = plain_ref[now, half:] + sign * plain_ref[prior, :half]


def pair_sums(out_ref, one_ref, lag_ref, chans, panels, forward):
    half = out_ref.shape[1] // 2
    group = 4
    for lane in range(0, half, 128):

        def step(row, carry):
            start = pl.multiple_of(row * 8, 8)

            def load(ref, panel):
                rows = pl.ds(panel * chans + start, 8)
                return ref[rows, lane : lane + 128], ref[rows, half + lane : half + lane + 128]

            for first in range(0, panels, group):
                sums = [None] * group
                ones = {}
                lags = range(first + group) if forward else range(panels - first)
                for lag in lags:
                    lag_re, lag_im = load(lag_ref, lag)
                    for at in range(group):
                        other = first + at - lag if forward else first + at + lag
                        if not 0 <= other < panels:
                            continue
                        if other not in ones:
                            ones[other] = load(one_ref, other)
                        one_re, one_im = ones[other]
                        if forward:
                            re = one_re * lag_re - one_im * lag_im
                            im = one_re * lag_im + one_im * lag_re
                        else:
                            re = one_re * lag_re + one_im * lag_im
                            im = one_im * lag_re - one_re * lag_im
                        held = sums[at]
                        sums[at] = (re, im) if held is None else (held[0] + re, held[1] + im)
                for at in range(group):
                    rows = pl.ds((first + at) * chans + start, 8)
                    out_ref[rows, lane : lane + 128] = sums[at][0]
                    out_ref[rows, half + lane : half + lane + 128] = sums[at][1]
            return carry

        lax.fori_loop(0, chans // 8, step, 0)


def by_rows(ref, at, chans):
    part = ref[:, at * chans : (at + 1) * chans, :]
    return part.reshape(part.shape[0] * chans, part.shape[2])


def send_kernel(panels, signal_ref, gate_ref, grad_ref, filter_ref, out_ref):
    chans = out_ref.shape[1] // 3

    def put(at, panel):
        parts = panel.T.reshape(panels, chans, panel.shape[0])
        out_ref[:, at * chans : (at + 1) * chans, :] = parts

    gated = gate_ref[...].astype(jnp.float32) * grad_ref[...].astype(jnp.float32)
    put(0, gated.astype(jnp.bfloat16))
    put(1, filter_ref[...])
    put(2, signal_ref[...])


def signal_grad_kernel(
    panels, parts_ref, high_ref, low_ref, grad_ref, gated_spec, filter_full, plain, sums
):
    chans = parts_ref.shape[1] // 3
    gated_spec[...] = spectra(by_rows(parts_ref, 0, chans), high_ref, low_ref)
    plain[...] = spectra(by_rows(parts_ref, 1, chans), high_ref, low_ref)
    widen(plain, filter_full, chans, panels)
    pair_sums(sums, gated_spec, filter_full, chans, panels, False)
    grad_ref[...] = inverse(sums[...], high_ref, low_ref).astype(grad_ref.dtype)


def rest_kernel(
    panels, parts_ref, gated_spec, filter_full, high_ref, low_ref, out_ref, plain, full, sums
):
    chans = parts_ref.shape[1] // 3

    def put(at):
        grad = inverse(sums[...], high_ref, low_ref).astype(out_ref.dtype)
        out_ref[:, at * chans : (at + 1) * chans, :] = grad.reshape(panels, chans, grad.shape[1])

    plain[...] = spectra(by_rows(parts_ref, 2, chans), high_ref, low_ref)
    widen(plain, full, chans, panels)
    pair_sums(sums, plain, filter_full, chans, panels, True)
    put(0)
    pair_sums(sums, gated_spec, full, chans, panels, False)
    put(1)


def finish_kernel(panels, parts_ref, grad_ref, gate_out, filter_out):
    chans = parts_ref.shape[1] // 2
    conv = by_rows(parts_ref, 0, chans).T.astype(jnp.float32)
    gate_out[...] = (grad_ref[...].astype(jnp.float32) * conv).astype(gate_out.dtype)
    filter_out[...] = by_rows(parts_ref, 1, chans).T.astype(jnp.float32)


def whole(count):
    return [pl.BlockSpec(memory_space=pltpu.VMEM)] * count


def call(kernel, panels, outs, scratch, *operands):
    return pl.pallas_call(
        lambda *refs: kernel(panels, *refs),
        out_shape=outs,
        in_specs=whole(len(operands)),
        out_specs=whole(len(outs)),
        scratch_shapes=scratch,
        compiler_params=pltpu.CompilerParams(vmem_limit_bytes=40 * 1024 * 1024),
    )(*operands)


def shifted(x, axis, by):
    length = lax.axis_size(axis)
    return lax.ppermute(x, axis, [(i, (i + by) % length) for i in range(length)])


def on_device(signal, gate_value, grad_out, long_filter, weight):
    panel_len, width = signal.shape[1:]
    panels = lax.axis_size("seq")
    groups = lax.axis_size("chan")
    chans = width // panels
    rows = panels * chans
    high, low = make_tables(panel_len)
    high, low = jnp.asarray(high), jnp.asarray(low)

    def swapped(parts):
        return lax.all_to_all(parts, "seq", 0, 0, tiled=True)

    def shape(*dims, dtype=jnp.bfloat16):
        return jax.ShapeDtypeStruct(dims, dtype)

    (sent,) = call(
        send_kernel,
        panels,
        (shape(panels, 3 * chans, panel_len),),
        [],
        signal[0],
        gate_value[0],
        grad_out[0],
        long_filter[0],
    )
    parts = swapped(sent)

    my_group = lax.axis_index("chan")
    weight_parts = weight[0].reshape(groups, weight.shape[1] // groups, width)

    def weight_for(by):
        return lax.dynamic_index_in_dim(
            weight_parts, lax.rem(my_group + by, groups), 0, False
        )

    weights = [weight_for(0)] + [shifted(weight_for(by), "chan", by) for by in range(1, groups)]

    parts, weights[1], weights[-1] = lax.optimization_barrier((parts, weights[1], weights[-1]))

    spec = shape(rows, 2 * panel_len, dtype=jnp.float32)
    held = pltpu.VMEM((rows, 2 * panel_len), jnp.float32)
    signal_grad, gated_spec, filter_full = call(
        signal_grad_kernel,
        panels,
        (shape(rows, panel_len), spec, spec),
        [held, held],
        parts,
        high,
        low,
    )
    signal_grad = swapped(signal_grad.reshape(panels, chans, panel_len)).reshape(width, panel_len)
    (rest,) = call(
        rest_kernel,
        panels,
        (shape(panels, 2 * chans, panel_len),),
        [held, held, held],
        parts,
        gated_spec,
        filter_full,
        high,
        low,
    )
    signal_grad, rest, weights[2] = lax.optimization_barrier((signal_grad, rest, weights[2]))
    received = shifted(signal_grad, "pipe", -1)
    rest = swapped(rest)
    total = 0.0
    for by in range(groups):
        held_by = received if by == 0 else shifted(received, "chan", by)
        total = total + lax.dot_general(
            held_by, weights[by], (((0,), (1,)), ((), ())), preferred_element_type=jnp.float32
        )
    input_grad = total.astype(jnp.bfloat16)
    gate_grad, filter_grad = call(
        finish_kernel,
        panels,
        (shape(panel_len, width), shape(panel_len, width, dtype=jnp.float32)),
        [],
        rest,
        grad_out[0],
    )
    return gate_grad[None], filter_grad[None], input_grad[None]


def solution(mesh):
    return jax.shard_map(
        on_device,
        mesh=mesh,
        in_specs=(
            P("pipe", "seq", "chan"),
            P("pipe", "seq", "chan"),
            P("pipe", "seq", "chan"),
            P("pipe", "seq", "chan"),
            P("pipe", None, "chan"),
        ),
        out_specs=(P("pipe", "seq", "chan"), P("pipe", "seq", "chan"), P("pipe", "seq", "chan")),
        check_vma=False,
    )
```

```python
import jax
import jax.numpy as jnp
import ml_dtypes
import numpy as np
from jax import lax
from jax.experimental import pallas as pl
from jax.experimental.pallas import tpu as pltpu
from jax.sharding import PartitionSpec as P


def make_tables(panel_len):
    position = np.arange(panel_len)[:, None]
    odd = 2 * np.arange(panel_len)[None, :] + 1
    angles = (position * odd % (4 * panel_len)) * (np.pi / (2 * panel_len))
    table = np.concatenate([np.cos(angles), -np.sin(angles)], axis=1)
    high = table.astype(np.float32).astype(ml_dtypes.bfloat16)
    low = (table - high.astype(np.float64)).astype(np.float32).astype(ml_dtypes.bfloat16)
    return high, low


def dot(left, right):
    return jnp.dot(left, right, preferred_element_type=jnp.float32)


def spectra(rows, high_ref, low_ref):
    return dot(rows, high_ref[...]) + dot(rows, low_ref[...])


def inverse(spec, high_ref, low_ref):
    panel_len = high_ref.shape[0]
    top = spec.astype(jnp.bfloat16)
    rest = (spec - top.astype(jnp.float32)).astype(jnp.bfloat16)
    dims = (((1,), (1,)), ((), ()))

    def back(left, right):
        return lax.dot_general(left, right, dims, preferred_element_type=jnp.float32)

    high = high_ref[...]
    return (back(top, high) + (back(rest, high) + back(top, low_ref[...]))) * (1.0 / panel_len)


def widen(plain_ref, full_ref, chans, panels):
    half = plain_ref.shape[1] // 2
    sign = 1.0 - 2.0 * (lax.broadcasted_iota(jnp.int32, (chans, half), 1) % 2).astype(jnp.float32)
    full_ref[pl.ds(0, chans), :] = plain_ref[pl.ds(0, chans), :]
    for panel in range(1, panels):
        now, prior = pl.ds(panel * chans, chans), pl.ds((panel - 1) * chans, chans)
        full_ref[now, :half] = plain_ref[now, :half] - sign * plain_ref[prior, half:]
        full_ref[now, half:] = plain_ref[now, half:] + sign * plain_ref[prior, :half]


def pair_sums(out_ref, one_ref, lag_ref, chans, panels, forward):
    half = out_ref.shape[1] // 2
    group = 4
    for lane in range(0, half, 128):

        def step(row, carry):
            start = pl.multiple_of(row * 8, 8)

            def load(ref, panel):
                rows = pl.ds(panel * chans + start, 8)
                return ref[rows, lane : lane + 128], ref[rows, half + lane : half + lane + 128]

            for first in range(0, panels, group):
                sums = [None] * group
                ones = {}
                lags = range(first + group) if forward else range(panels - first)
                for lag in lags:
                    lag_re, lag_im = load(lag_ref, lag)
                    for at in range(group):
                        other = first + at - lag if forward else first + at + lag
                        if not 0 <= other < panels:
                            continue
                        if other not in ones:
                            ones[other] = load(one_ref, other)
                        one_re, one_im = ones[other]
                        if forward:
                            re = one_re * lag_re - one_im * lag_im
                            im = one_re * lag_im + one_im * lag_re
                        else:
                            re = one_re * lag_re + one_im * lag_im
                            im = one_im * lag_re - one_re * lag_im
                        held = sums[at]
                        sums[at] = (re, im) if held is None else (held[0] + re, held[1] + im)
                for at in range(group):
                    rows = pl.ds((first + at) * chans + start, 8)
                    out_ref[rows, lane : lane + 128] = sums[at][0]
                    out_ref[rows, half + lane : half + lane + 128] = sums[at][1]
            return carry

        lax.fori_loop(0, chans // 8, step, 0)


def by_rows(ref, at, chans):
    part = ref[:, at * chans : (at + 1) * chans, :]
    return part.reshape(part.shape[0] * chans, part.shape[2])


def send_kernel(
    panels, signal_in, gate_in, grad_in, filter_in, out_ref, signal_ref, gate_ref, grad_ref, filter_ref, sems
):
    chans = out_ref.shape[1] // 3
    copies = []
    for at, (source, target) in enumerate(
        ((gate_in, gate_ref), (grad_in, grad_ref), (filter_in, filter_ref), (signal_in, signal_ref))
    ):
        copies.append(pltpu.make_async_copy(source, target, sems.at[at]))
        copies[-1].start()

    def put(at, panel):
        parts = panel.T.reshape(panels, chans, panel.shape[0])
        out_ref[:, at * chans : (at + 1) * chans, :] = parts

    copies[0].wait()
    copies[1].wait()
    gated = gate_ref[...].astype(jnp.float32) * grad_ref[...].astype(jnp.float32)
    put(0, gated.astype(jnp.bfloat16))
    copies[2].wait()
    put(1, filter_ref[...])
    copies[3].wait()
    put(2, signal_ref[...])


def signal_grad_kernel(
    panels, parts_ref, high_ref, low_ref, grad_ref, gated_spec, filter_full, plain, sums
):
    chans = parts_ref.shape[1] // 3
    gated_spec[...] = spectra(by_rows(parts_ref, 0, chans), high_ref, low_ref)
    plain[...] = spectra(by_rows(parts_ref, 1, chans), high_ref, low_ref)
    widen(plain, filter_full, chans, panels)
    pair_sums(sums, gated_spec, filter_full, chans, panels, False)
    grad_ref[...] = inverse(sums[...], high_ref, low_ref).astype(grad_ref.dtype)


def rest_kernel(
    panels, parts_ref, gated_spec, filter_full, high_ref, low_ref, out_ref, plain, full, sums
):
    chans = parts_ref.shape[1] // 3

    def put(at):
        grad = inverse(sums[...], high_ref, low_ref).astype(out_ref.dtype)
        out_ref[:, at * chans : (at + 1) * chans, :] = grad.reshape(panels, chans, grad.shape[1])

    plain[...] = spectra(by_rows(parts_ref, 2, chans), high_ref, low_ref)
    widen(plain, full, chans, panels)
    pair_sums(sums, plain, filter_full, chans, panels, True)
    put(0)
    pair_sums(sums, gated_spec, full, chans, panels, False)
    put(1)


def finish_kernel(panels, parts_ref, grad_ref, gate_out, filter_out):
    chans = parts_ref.shape[1] // 2
    conv = by_rows(parts_ref, 0, chans).T.astype(jnp.float32)
    gate_out[...] = (grad_ref[...].astype(jnp.float32) * conv).astype(gate_out.dtype)
    filter_out[...] = by_rows(parts_ref, 1, chans).T.astype(jnp.float32)


def call(kernel, panels, outs, scratch, *operands, space=pltpu.VMEM):
    return pl.pallas_call(
        lambda *refs: kernel(panels, *refs),
        out_shape=outs,
        in_specs=[pl.BlockSpec(memory_space=space)] * len(operands),
        out_specs=[pl.BlockSpec(memory_space=pltpu.VMEM)] * len(outs),
        scratch_shapes=scratch,
        compiler_params=pltpu.CompilerParams(vmem_limit_bytes=40 * 1024 * 1024),
    )(*operands)


def shifted(x, axis, by):
    length = lax.axis_size(axis)
    return lax.ppermute(x, axis, [(i, (i + by) % length) for i in range(length)])


def on_device(signal, gate_value, grad_out, long_filter, weight):
    panel_len, width = signal.shape[1:]
    panels = lax.axis_size("seq")
    groups = lax.axis_size("chan")
    chans = width // panels
    rows = panels * chans
    high, low = make_tables(panel_len)
    high, low = jnp.asarray(high), jnp.asarray(low)

    def swapped(parts):
        return lax.all_to_all(parts, "seq", 0, 0, tiled=True)

    def shape(*dims, dtype=jnp.bfloat16):
        return jax.ShapeDtypeStruct(dims, dtype)

    (sent,) = call(
        send_kernel,
        panels,
        (shape(panels, 3 * chans, panel_len),),
        [pltpu.VMEM((panel_len, width), jnp.bfloat16)] * 4 + [pltpu.SemaphoreType.DMA((4,))],
        *(
            pltpu.with_memory_space_constraint(panel[0], pltpu.HBM)
            for panel in (signal, gate_value, grad_out, long_filter)
        ),
        space=pltpu.HBM,
    )
    parts = swapped(sent)

    my_group = lax.axis_index("chan")
    weight_parts = weight[0].reshape(groups, weight.shape[1] // groups, width)

    def weight_for(by):
        return lax.dynamic_index_in_dim(
            weight_parts, lax.rem(my_group + by, groups), 0, False
        )

    weights = [weight_for(0)] + [shifted(weight_for(by), "chan", by) for by in range(1, groups)]

    spec = shape(rows, 2 * panel_len, dtype=jnp.float32)
    held = pltpu.VMEM((rows, 2 * panel_len), jnp.float32)
    signal_grad, gated_spec, filter_full = call(
        signal_grad_kernel,
        panels,
        (pltpu.HBM((rows, panel_len), jnp.bfloat16), spec, spec),
        [held, held],
        parts,
        high,
        low,
    )
    signal_grad = swapped(signal_grad.reshape(panels, chans, panel_len)).reshape(width, panel_len)
    (rest,) = call(
        rest_kernel,
        panels,
        (shape(panels, 2 * chans, panel_len),),
        [held, held, held],
        parts,
        gated_spec,
        filter_full,
        high,
        low,
    )
    signal_grad, rest = lax.optimization_barrier((signal_grad, rest))
    received = shifted(signal_grad, "pipe", -1)
    rest = swapped(rest)
    received, weights = lax.optimization_barrier((received, weights))
    total = 0.0
    for by in range(groups):
        held_by = received if by == 0 else shifted(received, "chan", by)
        total = total + lax.dot_general(
            held_by, weights[by], (((0,), (1,)), ((), ())), preferred_element_type=jnp.float32
        )
    input_grad = total.astype(jnp.bfloat16)
    gate_grad, filter_grad = call(
        finish_kernel,
        panels,
        (shape(panel_len, width), shape(panel_len, width, dtype=jnp.float32)),
        [],
        rest,
        grad_out[0],
    )
    return gate_grad[None], filter_grad[None], input_grad[None]


def solution(mesh):
    return jax.shard_map(
        on_device,
        mesh=mesh,
        in_specs=(
            P("pipe", "seq", "chan"),
            P("pipe", "seq", "chan"),
            P("pipe", "seq", "chan"),
            P("pipe", "seq", "chan"),
            P("pipe", None, "chan"),
        ),
        out_specs=(P("pipe", "seq", "chan"), P("pipe", "seq", "chan"), P("pipe", "seq", "chan")),
        check_vma=False,
    )
```

```python
import jax
import jax.numpy as jnp
import ml_dtypes
import numpy as np
from jax import lax
from jax.experimental import pallas as pl
from jax.experimental.pallas import tpu as pltpu
from jax.sharding import PartitionSpec as P


def make_tables(panel_len):
    position = np.arange(panel_len)[:, None]
    odd = 2 * np.arange(panel_len)[None, :] + 1
    angles = (position * odd % (4 * panel_len)) * (np.pi / (2 * panel_len))
    table = np.concatenate([np.cos(angles), -np.sin(angles)], axis=1)
    high = table.astype(np.float32).astype(ml_dtypes.bfloat16)
    low = (table - high.astype(np.float64)).astype(np.float32).astype(ml_dtypes.bfloat16)
    return high, low


def dot(left, right):
    return jnp.dot(left, right, preferred_element_type=jnp.float32)


def spectra(rows, high_ref, low_ref):
    return dot(rows, high_ref[...]) + dot(rows, low_ref[...])


def inverse(spec, high_ref, low_ref):
    panel_len = high_ref.shape[0]
    top = spec.astype(jnp.bfloat16)
    rest = (spec - top.astype(jnp.float32)).astype(jnp.bfloat16)
    dims = (((1,), (1,)), ((), ()))

    def back(left, right):
        return lax.dot_general(left, right, dims, preferred_element_type=jnp.float32)

    high = high_ref[...]
    return (back(top, high) + (back(rest, high) + back(top, low_ref[...]))) * (1.0 / panel_len)


def widen(plain_ref, full_ref, chans, panels):
    half = plain_ref.shape[1] // 2
    sign = 1.0 - 2.0 * (lax.broadcasted_iota(jnp.int32, (chans, half), 1) % 2).astype(jnp.float32)
    full_ref[pl.ds(0, chans), :] = plain_ref[pl.ds(0, chans), :]
    for panel in range(1, panels):
        now, prior = pl.ds(panel * chans, chans), pl.ds((panel - 1) * chans, chans)
        full_ref[now, :half] = plain_ref[now, :half] - sign * plain_ref[prior, half:]
        full_ref[now, half:] = plain_ref[now, half:] + sign * plain_ref[prior, :half]


def pair_sums(out_ref, one_ref, lag_ref, chans, panels, forward):
    half = out_ref.shape[1] // 2
    group = 4
    for lane in range(0, half, 128):

        def step(row, carry):
            start = pl.multiple_of(row * 8, 8)

            def load(ref, panel):
                rows = pl.ds(panel * chans + start, 8)
                return ref[rows, lane : lane + 128], ref[rows, half + lane : half + lane + 128]

            for first in range(0, panels, group):
                sums = [None] * group
                ones = {}
                lags = range(first + group) if forward else range(panels - first)
                for lag in lags:
                    lag_re, lag_im = load(lag_ref, lag)
                    for at in range(group):
                        other = first + at - lag if forward else first + at + lag
                        if not 0 <= other < panels:
                            continue
                        if other not in ones:
                            ones[other] = load(one_ref, other)
                        one_re, one_im = ones[other]
                        if forward:
                            re = one_re * lag_re - one_im * lag_im
                            im = one_re * lag_im + one_im * lag_re
                        else:
                            re = one_re * lag_re + one_im * lag_im
                            im = one_im * lag_re - one_re * lag_im
                        held = sums[at]
                        sums[at] = (re, im) if held is None else (held[0] + re, held[1] + im)
                for at in range(group):
                    rows = pl.ds((first + at) * chans + start, 8)
                    out_ref[rows, lane : lane + 128] = sums[at][0]
                    out_ref[rows, half + lane : half + lane + 128] = sums[at][1]
            return carry

        lax.fori_loop(0, chans // 8, step, 0)


def by_rows(ref, at, chans):
    part = ref[:, at * chans : (at + 1) * chans, :]
    return part.reshape(part.shape[0] * chans, part.shape[2])


def send_kernel(
    panels, signal_in, gate_in, grad_in, filter_in, out_ref, signal_ref, gate_ref, grad_ref, filter_ref, sems
):
    chans = out_ref.shape[1] // 3
    copies = []
    for at, (source, target) in enumerate(
        ((gate_in, gate_ref), (grad_in, grad_ref), (filter_in, filter_ref), (signal_in, signal_ref))
    ):
        copies.append(pltpu.make_async_copy(source, target, sems.at[at]))
        copies[-1].start()

    def put(at, panel):
        parts = panel.T.reshape(panels, chans, panel.shape[0])
        out_ref[:, at * chans : (at + 1) * chans, :] = parts

    copies[0].wait()
    copies[1].wait()
    gated = gate_ref[...].astype(jnp.float32) * grad_ref[...].astype(jnp.float32)
    put(0, gated.astype(jnp.bfloat16))
    copies[2].wait()
    put(1, filter_ref[...])
    copies[3].wait()
    put(2, signal_ref[...])


def filter_spectra(parts_ref, high_ref, low_ref, gated_spec, filter_full, plain):
    panels, chans = parts_ref.shape[0], parts_ref.shape[1] // 3
    gated_spec[...] = spectra(by_rows(parts_ref, 0, chans), high_ref, low_ref)
    plain[...] = spectra(by_rows(parts_ref, 1, chans), high_ref, low_ref)
    widen(plain, filter_full, chans, panels)


def signal_grad_kernel(
    panels, parts_ref, high_ref, low_ref, grad_ref, gated_spec, filter_full, plain, sums
):
    chans = parts_ref.shape[1] // 3
    filter_spectra(parts_ref, high_ref, low_ref, gated_spec, filter_full, plain)
    pair_sums(sums, gated_spec, filter_full, chans, panels, False)
    grad_ref[...] = inverse(sums[...], high_ref, low_ref).astype(grad_ref.dtype)


def rest_kernel(
    panels, parts_ref, high_ref, low_ref, out_ref, gated_spec, filter_full, plain, full, sums
):
    chans = parts_ref.shape[1] // 3

    def put(at):
        grad = inverse(sums[...], high_ref, low_ref).astype(out_ref.dtype)
        out_ref[:, at * chans : (at + 1) * chans, :] = grad.reshape(panels, chans, grad.shape[1])

    filter_spectra(parts_ref, high_ref, low_ref, gated_spec, filter_full, plain)
    plain[...] = spectra(by_rows(parts_ref, 2, chans), high_ref, low_ref)
    widen(plain, full, chans, panels)
    pair_sums(sums, plain, filter_full, chans, panels, True)
    put(0)
    pair_sums(sums, gated_spec, full, chans, panels, False)
    put(1)


def finish_kernel(panels, parts_ref, grad_ref, gate_out, filter_out):
    chans = parts_ref.shape[1] // 2
    conv = by_rows(parts_ref, 0, chans).T.astype(jnp.float32)
    gate_out[...] = (grad_ref[...].astype(jnp.float32) * conv).astype(gate_out.dtype)
    filter_out[...] = by_rows(parts_ref, 1, chans).T.astype(jnp.float32)


def call(kernel, panels, outs, scratch, *operands, space=pltpu.VMEM):
    return pl.pallas_call(
        lambda *refs: kernel(panels, *refs),
        out_shape=outs,
        in_specs=[pl.BlockSpec(memory_space=space)] * len(operands),
        out_specs=[pl.BlockSpec(memory_space=pltpu.VMEM)] * len(outs),
        scratch_shapes=scratch,
        compiler_params=pltpu.CompilerParams(vmem_limit_bytes=16 * 1024 * 1024),
    )(*operands)


def shifted(x, axis, by):
    length = lax.axis_size(axis)
    return lax.ppermute(x, axis, [(i, (i + by) % length) for i in range(length)])


def on_device(signal, gate_value, grad_out, long_filter, weight):
    panel_len, width = signal.shape[1:]
    panels = lax.axis_size("seq")
    groups = lax.axis_size("chan")
    chans = width // panels
    rows = panels * chans
    high, low = make_tables(panel_len)
    high, low = jnp.asarray(high), jnp.asarray(low)

    def swapped(parts):
        return lax.all_to_all(parts, "seq", 0, 0, tiled=True)

    def shape(*dims, dtype=jnp.bfloat16):
        return jax.ShapeDtypeStruct(dims, dtype)

    (sent,) = call(
        send_kernel,
        panels,
        (pltpu.HBM((panels, 3 * chans, panel_len), jnp.bfloat16),),
        [pltpu.VMEM((panel_len, width), jnp.bfloat16)] * 4 + [pltpu.SemaphoreType.DMA((4,))],
        *(
            pltpu.with_memory_space_constraint(panel[0], pltpu.HBM)
            for panel in (signal, gate_value, grad_out, long_filter)
        ),
        space=pltpu.HBM,
    )
    parts = swapped(sent)

    my_group, my_half = lax.axis_index("chan"), lax.rem(lax.axis_index("seq"), 2)
    outputs = weight.shape[1] // groups
    weight_parts = weight[0].reshape(groups * 2, outputs // 2, width)
    pairs = [(i, i ^ 1) for i in range(panels)]

    def fetch(source, by):
        at = 2 * lax.rem(my_group + by, groups) + my_half
        return shifted(lax.dynamic_index_in_dim(source, at, 0, False), "chan", by)

    def pair_swap(part):
        return lax.ppermute(part, "seq", pairs)

    near = [fetch(weight_parts, by) for by in (1, groups - 1)]
    parts, near = lax.optimization_barrier((parts, near))

    held = pltpu.VMEM((rows, 2 * panel_len), jnp.float32)
    (signal_grad,) = call(
        signal_grad_kernel,
        panels,
        (pltpu.HBM((rows, panel_len), jnp.bfloat16),),
        [held] * 4,
        parts,
        high,
        low,
    )
    near, signal_grad = lax.optimization_barrier((near, signal_grad))
    near_others = [pair_swap(part) for part in near]
    weight_parts, _ = lax.optimization_barrier((weight_parts, near[0]))
    far = fetch(weight_parts, 2)
    signal_grad = swapped(signal_grad.reshape(panels, chans, panel_len)).reshape(width, panel_len)
    (rest,) = call(
        rest_kernel,
        panels,
        (pltpu.HBM((panels, 2 * chans, panel_len), jnp.bfloat16),),
        [held] * 5,
        parts,
        high,
        low,
    )
    signal_grad, rest, far, near_others = lax.optimization_barrier(
        (signal_grad, rest, far, near_others)
    )
    received = shifted(signal_grad, "pipe", -1)
    far_other = pair_swap(far)
    rest, far_other = lax.optimization_barrier((rest, far_other))
    received, far_other = lax.optimization_barrier((received, far_other))
    rest = swapped(rest)
    fetched = [near[0], far, near[1]]
    others = [near_others[0], far_other, near_others[1]]

    def project(block, block_weight):
        return lax.dot_general(
            block, block_weight, (((0,), (1,)), ((), ())), preferred_element_type=jnp.float32
        )

    gate_grad, filter_grad = call(
        finish_kernel,
        panels,
        (shape(panel_len, width), shape(panel_len, width, dtype=jnp.float32)),
        [],
        rest,
        grad_out[0],
    )
    total = project(received, lax.dynamic_slice_in_dim(weight[0], my_group * outputs, outputs, 0))
    for at, by in enumerate((1, 2, groups - 1)):
        ordered = jnp.where(
            my_half == 0,
            jnp.concatenate([fetched[at], others[at]]),
            jnp.concatenate([others[at], fetched[at]]),
        )
        block = shifted(received, "chan", by)
        block, ordered, total = lax.optimization_barrier((block, ordered, total))
        if at == 2:
            block, gate_grad, filter_grad = lax.optimization_barrier((block, gate_grad, filter_grad))
        total = total + project(block, ordered)
    input_grad = total.astype(jnp.bfloat16)
    return gate_grad[None], filter_grad[None], input_grad[None]


def solution(mesh):
    return jax.shard_map(
        on_device,
        mesh=mesh,
        in_specs=(
            P("pipe", "seq", "chan"),
            P("pipe", "seq", "chan"),
            P("pipe", "seq", "chan"),
            P("pipe", "seq", "chan"),
            P("pipe", None, "chan"),
        ),
        out_specs=(P("pipe", "seq", "chan"), P("pipe", "seq", "chan"), P("pipe", "seq", "chan")),
        check_vma=False,
    )
```

```python
import jax
import jax.numpy as jnp
import ml_dtypes
import numpy as np
from jax import lax
from jax.experimental import pallas as pl
from jax.experimental.pallas import tpu as pltpu
from jax.sharding import PartitionSpec as P


def make_tables(panel_len):
    position = np.arange(panel_len)[:, None]
    odd = 2 * np.arange(panel_len)[None, :] + 1
    angles = (position * odd % (4 * panel_len)) * (np.pi / (2 * panel_len))
    table = np.concatenate([np.cos(angles), -np.sin(angles)], axis=1)
    high = table.astype(np.float32).astype(ml_dtypes.bfloat16)
    low = (table - high.astype(np.float64)).astype(np.float32).astype(ml_dtypes.bfloat16)
    return high, low


def dot(left, right):
    return jnp.dot(left, right, preferred_element_type=jnp.float32)


def spectra(rows, high_ref, low_ref):
    return dot(rows, high_ref[...]) + dot(rows, low_ref[...])


def inverse(spec, high_ref, low_ref):
    panel_len = high_ref.shape[0]
    top = spec.astype(jnp.bfloat16)
    rest = (spec - top.astype(jnp.float32)).astype(jnp.bfloat16)
    dims = (((1,), (1,)), ((), ()))

    def back(left, right):
        return lax.dot_general(left, right, dims, preferred_element_type=jnp.float32)

    high = high_ref[...]
    return (back(top, high) + (back(rest, high) + back(top, low_ref[...]))) * (1.0 / panel_len)


def widen(plain_ref, full_ref, chans, panels):
    half = plain_ref.shape[1] // 2
    sign = 1.0 - 2.0 * (lax.broadcasted_iota(jnp.int32, (chans, half), 1) % 2).astype(jnp.float32)
    full_ref[pl.ds(0, chans), :] = plain_ref[pl.ds(0, chans), :]
    for panel in range(1, panels):
        now, prior = pl.ds(panel * chans, chans), pl.ds((panel - 1) * chans, chans)
        full_ref[now, :half] = plain_ref[now, :half] - sign * plain_ref[prior, half:]
        full_ref[now, half:] = plain_ref[now, half:] + sign * plain_ref[prior, :half]


def pair_sums(out_ref, one_ref, lag_ref, chans, panels, forward):
    half = out_ref.shape[1] // 2
    group = 4
    for lane in range(0, half, 128):

        def step(row, carry):
            start = pl.multiple_of(row * 8, 8)

            def load(ref, panel):
                rows = pl.ds(panel * chans + start, 8)
                return ref[rows, lane : lane + 128], ref[rows, half + lane : half + lane + 128]

            for first in range(0, panels, group):
                sums = [None] * group
                ones = {}
                lags = range(first + group) if forward else range(panels - first)
                for lag in lags:
                    lag_re, lag_im = load(lag_ref, lag)
                    for at in range(group):
                        other = first + at - lag if forward else first + at + lag
                        if not 0 <= other < panels:
                            continue
                        if other not in ones:
                            ones[other] = load(one_ref, other)
                        one_re, one_im = ones[other]
                        if forward:
                            re = one_re * lag_re - one_im * lag_im
                            im = one_re * lag_im + one_im * lag_re
                        else:
                            re = one_re * lag_re + one_im * lag_im
                            im = one_im * lag_re - one_re * lag_im
                        held = sums[at]
                        sums[at] = (re, im) if held is None else (held[0] + re, held[1] + im)
                for at in range(group):
                    rows = pl.ds((first + at) * chans + start, 8)
                    out_ref[rows, lane : lane + 128] = sums[at][0]
                    out_ref[rows, half + lane : half + lane + 128] = sums[at][1]
            return carry

        lax.fori_loop(0, chans // 8, step, 0)


def by_rows(ref, at, chans):
    part = ref[:, at * chans : (at + 1) * chans, :]
    return part.reshape(part.shape[0] * chans, part.shape[2])


def send_kernel(
    panels, signal_in, gate_in, grad_in, filter_in, out_ref, signal_ref, gate_ref, grad_ref, filter_ref, sems
):
    chans = out_ref.shape[1] // 3
    copies = []
    for at, (source, target) in enumerate(
        ((gate_in, gate_ref), (grad_in, grad_ref), (filter_in, filter_ref), (signal_in, signal_ref))
    ):
        copies.append(pltpu.make_async_copy(source, target, sems.at[at]))
        copies[-1].start()

    def put(at, panel):
        parts = panel.T.reshape(panels, chans, panel.shape[0])
        out_ref[:, at * chans : (at + 1) * chans, :] = parts

    copies[0].wait()
    copies[1].wait()
    gated = gate_ref[...].astype(jnp.float32) * grad_ref[...].astype(jnp.float32)
    put(0, gated.astype(jnp.bfloat16))
    copies[2].wait()
    put(1, filter_ref[...])
    copies[3].wait()
    put(2, signal_ref[...])


def signal_grad_kernel(
    panels, parts_ref, high_ref, low_ref, grad_ref, gated_spec, filter_full, plain, sums
):
    chans = parts_ref.shape[1] // 3
    gated_spec[...] = spectra(by_rows(parts_ref, 0, chans), high_ref, low_ref)
    plain[...] = spectra(by_rows(parts_ref, 1, chans), high_ref, low_ref)
    widen(plain, filter_full, chans, panels)
    pair_sums(sums, gated_spec, filter_full, chans, panels, False)
    grad_ref[...] = inverse(sums[...], high_ref, low_ref).astype(grad_ref.dtype)


def rest_kernel(
    panels, parts_ref, high_ref, low_ref, out_ref, gated_spec, signal_spec, filter_spec, full, sums
):
    chans = parts_ref.shape[1] // 3

    def put(at):
        grad = inverse(sums[...], high_ref, low_ref).astype(out_ref.dtype)
        out_ref[:, at * chans : (at + 1) * chans, :] = grad.reshape(panels, chans, grad.shape[1])

    for at, spec in enumerate((gated_spec, filter_spec, signal_spec)):
        spec[...] = spectra(by_rows(parts_ref, at, chans), high_ref, low_ref)
    widen(signal_spec, full, chans, panels)
    pair_sums(sums, filter_spec, full, chans, panels, True)
    put(0)
    pair_sums(sums, gated_spec, full, chans, panels, False)
    put(1)


def weight_kernel(starts_ref, weight_ref, *refs):
    outs, sems = refs[:-1], refs[-1]
    copies = []
    for at, out in enumerate(outs):
        rows = out.shape[0]
        start = pl.multiple_of(starts_ref[at], 256)
        copies.append(pltpu.make_async_copy(weight_ref.at[pl.ds(start, rows)], out, sems.at[at]))
        copies[-1].start()
    for copy in copies:
        copy.wait()


def finish_kernel(panels, parts_ref, grad_ref, token_ref, gate_out, filter_out):
    chans = parts_ref.shape[1] // 2
    conv = by_rows(parts_ref, 0, chans).T.astype(jnp.float32)
    gate_out[...] = (grad_ref[...].astype(jnp.float32) * conv).astype(gate_out.dtype)
    filter_out[...] = by_rows(parts_ref, 1, chans).T.astype(jnp.float32)


def call(kernel, panels, outs, scratch, *operands, space=pltpu.VMEM):
    return pl.pallas_call(
        lambda *refs: kernel(panels, *refs),
        out_shape=outs,
        in_specs=[pl.BlockSpec(memory_space=space)] * len(operands),
        out_specs=[pl.BlockSpec(memory_space=pltpu.VMEM)] * len(outs),
        scratch_shapes=scratch,
        compiler_params=pltpu.CompilerParams(vmem_limit_bytes=16 * 1024 * 1024),
    )(*operands)


def shifted(x, axis, by):
    length = lax.axis_size(axis)
    return lax.ppermute(x, axis, [(i, (i + by) % length) for i in range(length)])


def on_device(signal, gate_value, grad_out, long_filter, weight):
    panel_len, width = signal.shape[1:]
    panels = lax.axis_size("seq")
    groups = lax.axis_size("chan")
    chans = width // panels
    rows = panels * chans
    high, low = make_tables(panel_len)
    high, low = jnp.asarray(high), jnp.asarray(low)

    def swapped(parts):
        return lax.all_to_all(parts, "seq", 0, 0, tiled=True)

    def shape(*dims, dtype=jnp.bfloat16):
        return jax.ShapeDtypeStruct(dims, dtype)

    (sent,) = call(
        send_kernel,
        panels,
        (pltpu.HBM((panels, 3 * chans, panel_len), jnp.bfloat16),),
        [pltpu.VMEM((panel_len, width), jnp.bfloat16)] * 4 + [pltpu.SemaphoreType.DMA((4,))],
        *(
            pltpu.with_memory_space_constraint(panel[0], pltpu.HBM)
            for panel in (signal, gate_value, grad_out, long_filter)
        ),
        space=pltpu.HBM,
    )
    parts = swapped(sent)

    my_group = lax.axis_index("chan")
    outputs = weight.shape[1] // groups
    starts = [outputs * lax.rem(my_group + by, groups) for by in (1, 3, 2)]
    weight_parts = pl.pallas_call(
        weight_kernel,
        out_shape=[pltpu.HBM((outputs, width), jnp.bfloat16)] * 3,
        in_specs=[
            pl.BlockSpec(memory_space=pltpu.SMEM),
            pl.BlockSpec(memory_space=pltpu.HBM),
        ],
        out_specs=[pl.BlockSpec(memory_space=pltpu.HBM)] * 3,
        scratch_shapes=[pltpu.SemaphoreType.DMA((3,))],
    )(jnp.stack(starts), pltpu.with_memory_space_constraint(weight[0], pltpu.HBM))
    weights = [shifted(part, "chan", by) for part, by in zip(weight_parts, (1, 3, 2))]

    held = pltpu.VMEM((rows, 2 * panel_len), jnp.float32)
    (signal_grad,) = call(
        signal_grad_kernel,
        panels,
        (pltpu.HBM((rows, panel_len), jnp.bfloat16),),
        [held] * 4,
        parts,
        high,
        low,
    )
    signal_grad = swapped(signal_grad.reshape(panels, chans, panel_len)).reshape(width, panel_len)
    (rest,) = call(
        rest_kernel,
        panels,
        (pltpu.HBM((panels, 2 * chans, panel_len), jnp.bfloat16),),
        [held] * 5,
        parts,
        high,
        low,
    )
    signal_grad, rest = lax.optimization_barrier((signal_grad, rest))
    received = shifted(signal_grad, "pipe", -1)
    token = lax.ppermute(signal_grad[:16, :128], "seq", [(i, i ^ 1) for i in range(panels)])
    rest, token = lax.optimization_barrier((rest, token))
    rest = swapped(rest)
    received, weights = lax.optimization_barrier((received, weights))

    def project(block, block_weight):
        return lax.dot_general(
            block, block_weight, (((0,), (1,)), ((), ())), preferred_element_type=jnp.float32
        )

    gate_grad, filter_grad = call(
        finish_kernel,
        panels,
        (shape(panel_len, width), shape(panel_len, width, dtype=jnp.float32)),
        [],
        rest,
        grad_out[0],
        token,
    )
    total = project(received, lax.dynamic_slice_in_dim(weight[0], my_group * outputs, outputs, 0))
    for by, part in zip((1, 3, 2), weights):
        block = shifted(received, "chan", by)
        block, total = lax.optimization_barrier((block, total))
        if by == 2:
            block, gate_grad, filter_grad = lax.optimization_barrier((block, gate_grad, filter_grad))
        total = total + project(block, part)
    input_grad = total.astype(jnp.bfloat16)
    return gate_grad[None], filter_grad[None], input_grad[None]


def solution(mesh):
    return jax.shard_map(
        on_device,
        mesh=mesh,
        in_specs=(
            P("pipe", "seq", "chan"),
            P("pipe", "seq", "chan"),
            P("pipe", "seq", "chan"),
            P("pipe", "seq", "chan"),
            P("pipe", None, "chan"),
        ),
        out_specs=(P("pipe", "seq", "chan"), P("pipe", "seq", "chan"), P("pipe", "seq", "chan")),
        check_vma=False,
    )
```

```python
import jax
import jax.numpy as jnp
import ml_dtypes
import numpy as np
from jax import lax
from jax.experimental import pallas as pl
from jax.experimental.pallas import tpu as pltpu
from jax.sharding import PartitionSpec as P


def make_tables(panel_len):
    position = np.arange(panel_len)[:, None]
    odd = 2 * np.arange(panel_len)[None, :] + 1
    angles = (position * odd % (4 * panel_len)) * (np.pi / (2 * panel_len))
    table = np.concatenate([np.cos(angles), -np.sin(angles)], axis=1)
    high = table.astype(np.float32).astype(ml_dtypes.bfloat16)
    low = (table - high.astype(np.float64)).astype(np.float32).astype(ml_dtypes.bfloat16)
    return high, low


def dot(left, right):
    return jnp.dot(left, right, preferred_element_type=jnp.float32)


def spectra(rows, high_ref, low_ref):
    return dot(rows, high_ref[...]) + dot(rows, low_ref[...])


def inverse(spec, high_ref, low_ref):
    panel_len = high_ref.shape[0]
    top = spec.astype(jnp.bfloat16)
    rest = (spec - top.astype(jnp.float32)).astype(jnp.bfloat16)
    dims = (((1,), (1,)), ((), ()))

    def back(left, right):
        return lax.dot_general(left, right, dims, preferred_element_type=jnp.float32)

    high = high_ref[...]
    return (back(top, high) + (back(rest, high) + back(top, low_ref[...]))) * (1.0 / panel_len)


def widen(plain_ref, full_ref, chans, panels):
    half = plain_ref.shape[1] // 2
    sign = 1.0 - 2.0 * (lax.broadcasted_iota(jnp.int32, (chans, half), 1) % 2).astype(jnp.float32)
    full_ref[pl.ds(0, chans), :] = plain_ref[pl.ds(0, chans), :]
    for panel in range(1, panels):
        now, prior = pl.ds(panel * chans, chans), pl.ds((panel - 1) * chans, chans)
        full_ref[now, :half] = plain_ref[now, :half] - sign * plain_ref[prior, half:]
        full_ref[now, half:] = plain_ref[now, half:] + sign * plain_ref[prior, :half]


def pair_sums(out_ref, one_ref, lag_ref, chans, panels, forward):
    half = out_ref.shape[1] // 2
    group = 4
    for lane in range(0, half, 128):

        def step(row, carry):
            start = pl.multiple_of(row * 8, 8)

            def load(ref, panel):
                rows = pl.ds(panel * chans + start, 8)
                return ref[rows, lane : lane + 128], ref[rows, half + lane : half + lane + 128]

            for first in range(0, panels, group):
                sums = [None] * group
                ones = {}
                lags = range(first + group) if forward else range(panels - first)
                for lag in lags:
                    lag_re, lag_im = load(lag_ref, lag)
                    for at in range(group):
                        other = first + at - lag if forward else first + at + lag
                        if not 0 <= other < panels:
                            continue
                        if other not in ones:
                            ones[other] = load(one_ref, other)
                        one_re, one_im = ones[other]
                        if forward:
                            re = one_re * lag_re - one_im * lag_im
                            im = one_re * lag_im + one_im * lag_re
                        else:
                            re = one_re * lag_re + one_im * lag_im
                            im = one_im * lag_re - one_re * lag_im
                        held = sums[at]
                        sums[at] = (re, im) if held is None else (held[0] + re, held[1] + im)
                for at in range(group):
                    rows = pl.ds((first + at) * chans + start, 8)
                    out_ref[rows, lane : lane + 128] = sums[at][0]
                    out_ref[rows, half + lane : half + lane + 128] = sums[at][1]
            return carry

        lax.fori_loop(0, chans // 8, step, 0)


def by_rows(ref, at, chans):
    part = ref[:, at * chans : (at + 1) * chans, :]
    return part.reshape(part.shape[0] * chans, part.shape[2])


def send_kernel(
    panels, signal_in, gate_in, grad_in, filter_in, out_ref, signal_ref, gate_ref, grad_ref, filter_ref, sems
):
    chans = out_ref.shape[1] // 3
    copies = []
    for at, (source, target) in enumerate(
        ((gate_in, gate_ref), (grad_in, grad_ref), (filter_in, filter_ref), (signal_in, signal_ref))
    ):
        copies.append(pltpu.make_async_copy(source, target, sems.at[at]))
        copies[-1].start()

    def put(at, panel):
        parts = panel.T.reshape(panels, chans, panel.shape[0])
        out_ref[:, at * chans : (at + 1) * chans, :] = parts

    copies[0].wait()
    copies[1].wait()
    gated = gate_ref[...].astype(jnp.float32) * grad_ref[...].astype(jnp.float32)
    put(0, gated.astype(jnp.bfloat16))
    copies[2].wait()
    put(1, filter_ref[...])
    copies[3].wait()
    put(2, signal_ref[...])


def signal_grad_kernel(
    panels, parts_ref, high_ref, low_ref, grad_ref, gated_spec, filter_full, plain, sums
):
    chans = parts_ref.shape[1] // 3
    gated_spec[...] = spectra(by_rows(parts_ref, 0, chans), high_ref, low_ref)
    plain[...] = spectra(by_rows(parts_ref, 1, chans), high_ref, low_ref)
    widen(plain, filter_full, chans, panels)
    pair_sums(sums, gated_spec, filter_full, chans, panels, False)
    grad_ref[...] = inverse(sums[...], high_ref, low_ref).astype(grad_ref.dtype)


def rest_kernel(
    panels, parts_ref, high_ref, low_ref, out_ref, gated_spec, signal_spec, filter_spec, full, sums
):
    chans = parts_ref.shape[1] // 3

    def put(at):
        grad = inverse(sums[...], high_ref, low_ref).astype(out_ref.dtype)
        out_ref[:, at * chans : (at + 1) * chans, :] = grad.reshape(panels, chans, grad.shape[1])

    for at, spec in enumerate((gated_spec, filter_spec, signal_spec)):
        spec[...] = spectra(by_rows(parts_ref, at, chans), high_ref, low_ref)
    widen(signal_spec, full, chans, panels)
    pair_sums(sums, filter_spec, full, chans, panels, True)
    put(0)
    pair_sums(sums, gated_spec, full, chans, panels, False)
    put(1)


def weight_kernel(starts_ref, weight_ref, *refs):
    count = (len(refs) - 1) // 2
    outs, helds, sems = refs[:count], refs[count:-1], refs[-1]
    loads, stores = [], []
    for at in range(count):
        rows = outs[at].shape[0]
        start = pl.multiple_of(starts_ref[at], 256)
        loads.append(
            pltpu.make_async_copy(weight_ref.at[pl.ds(start, rows)], helds[at], sems.at[0, at])
        )
        stores.append(pltpu.make_async_copy(helds[at], outs[at], sems.at[1, at]))
        loads[at].start()
    for at in range(count):
        loads[at].wait()
        stores[at].start()
    for store in stores:
        store.wait()


def finish_kernel(panels, parts_ref, grad_ref, token_ref, gate_out, filter_out):
    chans = parts_ref.shape[1] // 2
    conv = by_rows(parts_ref, 0, chans).T.astype(jnp.float32)
    gate_out[...] = (grad_ref[...].astype(jnp.float32) * conv).astype(gate_out.dtype)
    filter_out[...] = by_rows(parts_ref, 1, chans).T.astype(jnp.float32)


def call(kernel, panels, outs, scratch, *operands, space=pltpu.VMEM):
    return pl.pallas_call(
        lambda *refs: kernel(panels, *refs),
        out_shape=outs,
        in_specs=[pl.BlockSpec(memory_space=space)] * len(operands),
        out_specs=[pl.BlockSpec(memory_space=pltpu.VMEM)] * len(outs),
        scratch_shapes=scratch,
        compiler_params=pltpu.CompilerParams(vmem_limit_bytes=16 * 1024 * 1024),
    )(*operands)


def shifted(x, axis, by):
    length = lax.axis_size(axis)
    return lax.ppermute(x, axis, [(i, (i + by) % length) for i in range(length)])


def on_device(signal, gate_value, grad_out, long_filter, weight):
    panel_len, width = signal.shape[1:]
    panels = lax.axis_size("seq")
    groups = lax.axis_size("chan")
    chans = width // panels
    rows = panels * chans
    high, low = make_tables(panel_len)
    high, low = jnp.asarray(high), jnp.asarray(low)

    def swapped(parts):
        return lax.all_to_all(parts, "seq", 0, 0, tiled=True)

    def shape(*dims, dtype=jnp.bfloat16):
        return jax.ShapeDtypeStruct(dims, dtype)

    (sent,) = call(
        send_kernel,
        panels,
        (pltpu.HBM((panels, 3 * chans, panel_len), jnp.bfloat16),),
        [pltpu.VMEM((panel_len, width), jnp.bfloat16)] * 4 + [pltpu.SemaphoreType.DMA((4,))],
        *(
            pltpu.with_memory_space_constraint(panel[0], pltpu.HBM)
            for panel in (signal, gate_value, grad_out, long_filter)
        ),
        space=pltpu.HBM,
    )
    parts = swapped(sent)

    my_group = lax.axis_index("chan")
    outputs = weight.shape[1] // groups
    starts = [outputs * lax.rem(my_group + by, groups) for by in (1, 3, 2)]
    weight_parts = pl.pallas_call(
        weight_kernel,
        out_shape=[pltpu.HBM((outputs, width), jnp.bfloat16)] * 3,
        in_specs=[
            pl.BlockSpec(memory_space=pltpu.SMEM),
            pl.BlockSpec(memory_space=pltpu.HBM),
        ],
        out_specs=[pl.BlockSpec(memory_space=pltpu.HBM)] * 3,
        scratch_shapes=[pltpu.VMEM((outputs, width), jnp.bfloat16)] * 3
        + [pltpu.SemaphoreType.DMA((2, 3))],
        compiler_params=pltpu.CompilerParams(vmem_limit_bytes=16 * 1024 * 1024),
    )(jnp.stack(starts), pltpu.with_memory_space_constraint(weight[0], pltpu.HBM))
    weights = [shifted(part, "chan", by) for part, by in zip(weight_parts, (1, 3, 2))]

    held = pltpu.VMEM((rows, 2 * panel_len), jnp.float32)
    (signal_grad,) = call(
        signal_grad_kernel,
        panels,
        (pltpu.HBM((rows, panel_len), jnp.bfloat16),),
        [held] * 4,
        parts,
        high,
        low,
    )
    signal_grad = swapped(signal_grad.reshape(panels, chans, panel_len)).reshape(width, panel_len)
    (rest,) = call(
        rest_kernel,
        panels,
        (pltpu.HBM((panels, 2 * chans, panel_len), jnp.bfloat16),),
        [held] * 5,
        parts,
        high,
        low,
    )
    signal_grad, rest = lax.optimization_barrier((signal_grad, rest))
    received = shifted(signal_grad, "pipe", -1)
    token = lax.ppermute(signal_grad[:16, :128], "seq", [(i, i ^ 1) for i in range(panels)])
    rest, token = lax.optimization_barrier((rest, token))
    rest = swapped(rest)
    received, weights = lax.optimization_barrier((received, weights))

    def project(block, block_weight):
        return lax.dot_general(
            block, block_weight, (((0,), (1,)), ((), ())), preferred_element_type=jnp.float32
        )

    gate_grad, filter_grad = call(
        finish_kernel,
        panels,
        (shape(panel_len, width), shape(panel_len, width, dtype=jnp.float32)),
        [],
        rest,
        grad_out[0],
        token,
    )
    total = project(received, lax.dynamic_slice_in_dim(weight[0], my_group * outputs, outputs, 0))
    for by, part in zip((1, 3, 2), weights):
        block = shifted(received, "chan", by)
        block, total = lax.optimization_barrier((block, total))
        if by == 2:
            block, gate_grad, filter_grad = lax.optimization_barrier((block, gate_grad, filter_grad))
        total = total + project(block, part)
    input_grad = total.astype(jnp.bfloat16)
    return gate_grad[None], filter_grad[None], input_grad[None]


def solution(mesh):
    return jax.shard_map(
        on_device,
        mesh=mesh,
        in_specs=(
            P("pipe", "seq", "chan"),
            P("pipe", "seq", "chan"),
            P("pipe", "seq", "chan"),
            P("pipe", "seq", "chan"),
            P("pipe", None, "chan"),
        ),
        out_specs=(P("pipe", "seq", "chan"), P("pipe", "seq", "chan"), P("pipe", "seq", "chan")),
        check_vma=False,
    )
```

```python
import jax
import jax.numpy as jnp
import ml_dtypes
import numpy as np
from jax import lax
from jax.experimental import pallas as pl
from jax.experimental.pallas import tpu as pltpu
from jax.sharding import PartitionSpec as P


HINT_SCALE = 14


def make_tables(panel_len):
    position = np.arange(panel_len)[:, None]
    odd = 2 * np.arange(panel_len)[None, :] + 1
    angles = (position * odd % (4 * panel_len)) * (np.pi / (2 * panel_len))
    table = np.concatenate([np.cos(angles), -np.sin(angles)], axis=1)
    high = table.astype(np.float32).astype(ml_dtypes.bfloat16)
    low = (table - high.astype(np.float64)).astype(np.float32).astype(ml_dtypes.bfloat16)
    return high, low


def dot(left, right):
    return jnp.dot(left, right, preferred_element_type=jnp.float32)


def spectra(rows, high_ref, low_ref):
    return dot(rows, high_ref[...]) + dot(rows, low_ref[...])


def inverse(spec, high_ref, low_ref):
    panel_len = high_ref.shape[0]
    top = spec.astype(jnp.bfloat16)
    rest = (spec - top.astype(jnp.float32)).astype(jnp.bfloat16)
    dims = (((1,), (1,)), ((), ()))

    def back(left, right):
        return lax.dot_general(left, right, dims, preferred_element_type=jnp.float32)

    high = high_ref[...]
    return (back(top, high) + (back(rest, high) + back(top, low_ref[...]))) * (1.0 / panel_len)


def widen(plain_ref, full_ref, chans, panels):
    half = plain_ref.shape[1] // 2
    sign = 1.0 - 2.0 * (lax.broadcasted_iota(jnp.int32, (chans, half), 1) % 2).astype(jnp.float32)
    full_ref[pl.ds(0, chans), :] = plain_ref[pl.ds(0, chans), :]
    for panel in range(1, panels):
        now, prior = pl.ds(panel * chans, chans), pl.ds((panel - 1) * chans, chans)
        full_ref[now, :half] = plain_ref[now, :half] - sign * plain_ref[prior, half:]
        full_ref[now, half:] = plain_ref[now, half:] + sign * plain_ref[prior, :half]


def pair_sums(out_ref, one_ref, lag_ref, chans, panels, forward):
    half = out_ref.shape[1] // 2
    group = 4
    for lane in range(0, half, 128):

        def step(row, carry):
            start = pl.multiple_of(row * 8, 8)

            def load(ref, panel):
                rows = pl.ds(panel * chans + start, 8)
                return ref[rows, lane : lane + 128], ref[rows, half + lane : half + lane + 128]

            for first in range(0, panels, group):
                sums = [None] * group
                ones = {}
                lags = range(first + group) if forward else range(panels - first)
                for lag in lags:
                    lag_re, lag_im = load(lag_ref, lag)
                    for at in range(group):
                        other = first + at - lag if forward else first + at + lag
                        if not 0 <= other < panels:
                            continue
                        if other not in ones:
                            ones[other] = load(one_ref, other)
                        one_re, one_im = ones[other]
                        if forward:
                            re = one_re * lag_re - one_im * lag_im
                            im = one_re * lag_im + one_im * lag_re
                        else:
                            re = one_re * lag_re + one_im * lag_im
                            im = one_im * lag_re - one_re * lag_im
                        held = sums[at]
                        sums[at] = (re, im) if held is None else (held[0] + re, held[1] + im)
                for at in range(group):
                    rows = pl.ds((first + at) * chans + start, 8)
                    out_ref[rows, lane : lane + 128] = sums[at][0]
                    out_ref[rows, half + lane : half + lane + 128] = sums[at][1]
            return carry

        lax.fori_loop(0, chans // 8, step, 0)


def by_rows(ref, at, chans):
    part = ref[:, at * chans : (at + 1) * chans, :]
    return part.reshape(part.shape[0] * chans, part.shape[2])


def send_kernel(
    panels, signal_in, gate_in, grad_in, filter_in, out_ref, signal_ref, gate_ref, grad_ref, filter_ref, sems
):
    chans = out_ref.shape[1] // 3
    copies = []
    for at, (source, target) in enumerate(
        ((gate_in, gate_ref), (grad_in, grad_ref), (filter_in, filter_ref), (signal_in, signal_ref))
    ):
        copies.append(pltpu.make_async_copy(source, target, sems.at[at]))
        copies[-1].start()

    def put(at, panel):
        parts = panel.T.reshape(panels, chans, panel.shape[0])
        out_ref[:, at * chans : (at + 1) * chans, :] = parts

    copies[0].wait()
    copies[1].wait()
    gated = gate_ref[...].astype(jnp.float32) * grad_ref[...].astype(jnp.float32)
    put(0, gated.astype(jnp.bfloat16))
    copies[2].wait()
    put(1, filter_ref[...])
    copies[3].wait()
    put(2, signal_ref[...])


def signal_grad_kernel(
    panels, parts_ref, high_ref, low_ref, grad_ref, gated_spec, filter_full, plain, sums
):
    chans = parts_ref.shape[1] // 3
    gated_spec[...] = spectra(by_rows(parts_ref, 0, chans), high_ref, low_ref)
    plain[...] = spectra(by_rows(parts_ref, 1, chans), high_ref, low_ref)
    widen(plain, filter_full, chans, panels)
    pair_sums(sums, gated_spec, filter_full, chans, panels, False)
    grad_ref[...] = inverse(sums[...], high_ref, low_ref).astype(grad_ref.dtype)


def rest_kernel(
    panels, parts_ref, high_ref, low_ref, out_ref, gated_spec, signal_spec, filter_spec, full, sums
):
    chans = parts_ref.shape[1] // 3

    def put(at):
        grad = inverse(sums[...], high_ref, low_ref).astype(out_ref.dtype)
        out_ref[:, at * chans : (at + 1) * chans, :] = grad.reshape(panels, chans, grad.shape[1])

    for at, spec in enumerate((gated_spec, filter_spec, signal_spec)):
        spec[...] = spectra(by_rows(parts_ref, at, chans), high_ref, low_ref)
    widen(signal_spec, full, chans, panels)
    pair_sums(sums, filter_spec, full, chans, panels, True)
    put(0)
    pair_sums(sums, gated_spec, full, chans, panels, False)
    put(1)


def weight_kernel(starts_ref, weight_ref, *refs):
    count = (len(refs) - 1) // 2
    outs, helds, sems = refs[:count], refs[count:-1], refs[-1]
    loads, stores = [], []
    for at in range(count):
        rows = outs[at].shape[0]
        start = pl.multiple_of(starts_ref[at], 256)
        loads.append(
            pltpu.make_async_copy(weight_ref.at[pl.ds(start, rows)], helds[at], sems.at[0, at])
        )
        stores.append(pltpu.make_async_copy(helds[at], outs[at], sems.at[1, at]))
        loads[at].start()
    for at in range(count):
        loads[at].wait()
        stores[at].start()
    for store in stores:
        store.wait()


def finish_kernel(panels, parts_ref, grad_ref, token_ref, gate_out, filter_out):
    chans = parts_ref.shape[1] // 2
    conv = by_rows(parts_ref, 0, chans).T.astype(jnp.float32)
    gate_out[...] = (grad_ref[...].astype(jnp.float32) * conv).astype(gate_out.dtype)
    filter_out[...] = by_rows(parts_ref, 1, chans).T.astype(jnp.float32)


def project_kernel(panels, *refs):
    count = (len(refs) - 3) // 3
    total_ref, blocks, weights = refs[0], refs[1 : 1 + count], refs[1 + count : 1 + 2 * count]
    out_ref, held, sems = refs[1 + 2 * count], refs[2 + 2 * count : -1], refs[-1]
    copies = [pltpu.make_async_copy(weights[at], held[at], sems.at[at]) for at in range(count)]
    for copy in copies:
        copy.start()
    total = total_ref[...]
    for at in range(count):
        block = blocks[at][...].T
        copies[at].wait()
        total = total + lax.dot_general(
            block, held[at][...], (((1,), (1,)), ((), ())), preferred_element_type=jnp.float32
        )
    out_ref[...] = total.astype(out_ref.dtype)


def call(kernel, panels, outs, scratch, *operands, space=pltpu.VMEM, streamed=0, cost=None):
    return pl.pallas_call(
        lambda *refs: kernel(panels, *refs),
        out_shape=outs,
        in_specs=[pl.BlockSpec(memory_space=space)] * (len(operands) - streamed)
        + [pl.BlockSpec(memory_space=pltpu.HBM)] * streamed,
        out_specs=[pl.BlockSpec(memory_space=pltpu.VMEM)] * len(outs),
        scratch_shapes=scratch,
        cost_estimate=cost,
        compiler_params=pltpu.CompilerParams(vmem_limit_bytes=16 * 1024 * 1024),
    )(*operands)


def shifted(x, axis, by):
    length = lax.axis_size(axis)
    return lax.ppermute(x, axis, [(i, (i + by) % length) for i in range(length)])


def on_device(signal, gate_value, grad_out, long_filter, weight):
    panel_len, width = signal.shape[1:]
    panels = lax.axis_size("seq")
    groups = lax.axis_size("chan")
    chans = width // panels
    rows = panels * chans
    high, low = make_tables(panel_len)
    high, low = jnp.asarray(high), jnp.asarray(low)

    def swapped(parts):
        return lax.all_to_all(parts, "seq", 0, 0, tiled=True)

    def shape(*dims, dtype=jnp.bfloat16):
        return jax.ShapeDtypeStruct(dims, dtype)

    (sent,) = call(
        send_kernel,
        panels,
        (pltpu.HBM((panels, 3 * chans, panel_len), jnp.bfloat16),),
        [pltpu.VMEM((panel_len, width), jnp.bfloat16)] * 4 + [pltpu.SemaphoreType.DMA((4,))],
        *(
            pltpu.with_memory_space_constraint(panel[0], pltpu.HBM)
            for panel in (signal, gate_value, grad_out, long_filter)
        ),
        space=pltpu.HBM,
    )
    parts = swapped(sent)

    my_group = lax.axis_index("chan")
    outputs = weight.shape[1] // groups
    starts = [outputs * lax.rem(my_group + by, groups) for by in (1, 3, 2)]
    weight_parts = pl.pallas_call(
        weight_kernel,
        out_shape=[pltpu.HBM((outputs, width), jnp.bfloat16)] * 3,
        in_specs=[
            pl.BlockSpec(memory_space=pltpu.SMEM),
            pl.BlockSpec(memory_space=pltpu.HBM),
        ],
        out_specs=[pl.BlockSpec(memory_space=pltpu.HBM)] * 3,
        scratch_shapes=[pltpu.VMEM((outputs, width), jnp.bfloat16)] * 3
        + [pltpu.SemaphoreType.DMA((2, 3))],
        compiler_params=pltpu.CompilerParams(vmem_limit_bytes=16 * 1024 * 1024),
    )(jnp.stack(starts), pltpu.with_memory_space_constraint(weight[0], pltpu.HBM))
    weights = [shifted(part, "chan", by) for part, by in zip(weight_parts, (1, 3, 2))]

    held = pltpu.VMEM((rows, 2 * panel_len), jnp.float32)
    (signal_grad,) = call(
        signal_grad_kernel,
        panels,
        (pltpu.HBM((rows, panel_len), jnp.bfloat16),),
        [held] * 4,
        parts,
        high,
        low,
    )
    signal_grad = swapped(signal_grad.reshape(panels, chans, panel_len)).reshape(width, panel_len)
    (rest,) = call(
        rest_kernel,
        panels,
        (pltpu.HBM((panels, 2 * chans, panel_len), jnp.bfloat16),),
        [held] * 5,
        parts,
        high,
        low,
    )
    signal_grad, rest = lax.optimization_barrier((signal_grad, rest))
    received = shifted(signal_grad, "pipe", -1)
    token = lax.ppermute(signal_grad[:16, :128], "seq", [(i, i ^ 1) for i in range(panels)])
    rest, token = lax.optimization_barrier((rest, token))
    rest = swapped(rest)
    received, weights = lax.optimization_barrier((received, weights))

    def project(block, block_weight):
        return lax.dot_general(
            block, block_weight, (((0,), (1,)), ((), ())), preferred_element_type=jnp.float32
        )

    gate_grad, filter_grad = call(
        finish_kernel,
        panels,
        (shape(panel_len, width), shape(panel_len, width, dtype=jnp.float32)),
        [],
        rest,
        grad_out[0],
        token,
    )
    total = project(received, lax.dynamic_slice_in_dim(weight[0], my_group * outputs, outputs, 0))
    blocks = [shifted(received, "chan", by) for by in (1, 3, 2)]

    def add_blocks(total, which, dtype):
        count = len(which)
        (added,) = call(
            project_kernel,
            panels,
            (shape(panel_len, outputs, dtype=dtype),),
            [pltpu.VMEM((outputs, width), jnp.bfloat16)] * count
            + [pltpu.SemaphoreType.DMA((count,))],
            total,
            *(blocks[at] for at in which),
            *(pltpu.with_memory_space_constraint(weights[at], pltpu.HBM) for at in which),
            streamed=count,
            cost=pl.CostEstimate(
                flops=HINT_SCALE * 2 * count * panel_len * width * outputs,
                transcendentals=0,
                bytes_accessed=HINT_SCALE * 2 * count * outputs * width,
            ),
        )
        return added

    blocks[:2], total = lax.optimization_barrier((blocks[:2], total))
    total = add_blocks(total, (0, 1), jnp.float32)
    blocks[2], total, gate_grad, filter_grad = lax.optimization_barrier(
        (blocks[2], total, gate_grad, filter_grad)
    )
    input_grad = add_blocks(total, (2,), jnp.bfloat16)
    return gate_grad[None], filter_grad[None], input_grad[None]


def solution(mesh):
    return jax.shard_map(
        on_device,
        mesh=mesh,
        in_specs=(
            P("pipe", "seq", "chan"),
            P("pipe", "seq", "chan"),
            P("pipe", "seq", "chan"),
            P("pipe", "seq", "chan"),
            P("pipe", None, "chan"),
        ),
        out_specs=(P("pipe", "seq", "chan"), P("pipe", "seq", "chan"), P("pipe", "seq", "chan")),
        check_vma=False,
    )
```

```python
import jax
import jax.numpy as jnp
import ml_dtypes
import numpy as np
from jax import lax
from jax.experimental import pallas as pl
from jax.experimental.pallas import tpu as pltpu
from jax.sharding import PartitionSpec as P


HINT_SCALE = 14


def make_tables(panel_len):
    position = np.arange(panel_len)[:, None]
    odd = 2 * np.arange(panel_len)[None, :] + 1
    angles = (position * odd % (4 * panel_len)) * (np.pi / (2 * panel_len))
    table = np.concatenate([np.cos(angles), -np.sin(angles)], axis=1)
    high = table.astype(np.float32).astype(ml_dtypes.bfloat16)
    low = (table - high.astype(np.float64)).astype(np.float32).astype(ml_dtypes.bfloat16)
    return high, low


def dot(left, right):
    return jnp.dot(left, right, preferred_element_type=jnp.float32)


def spectra(rows, high_ref, low_ref):
    return dot(rows, high_ref[...]) + dot(rows, low_ref[...])


def inverse(spec, high_ref, low_ref):
    panel_len = high_ref.shape[0]
    top = spec.astype(jnp.bfloat16)
    rest = (spec - top.astype(jnp.float32)).astype(jnp.bfloat16)
    dims = (((1,), (1,)), ((), ()))

    def back(left, right):
        return lax.dot_general(left, right, dims, preferred_element_type=jnp.float32)

    high = high_ref[...]
    return (back(top, high) + (back(rest, high) + back(top, low_ref[...]))) * (1.0 / panel_len)


def widen(plain_ref, full_ref, chans, panels):
    half = plain_ref.shape[1] // 2
    sign = 1.0 - 2.0 * (lax.broadcasted_iota(jnp.int32, (chans, half), 1) % 2).astype(jnp.float32)
    full_ref[pl.ds(0, chans), :] = plain_ref[pl.ds(0, chans), :]
    for panel in range(1, panels):
        now, prior = pl.ds(panel * chans, chans), pl.ds((panel - 1) * chans, chans)
        full_ref[now, :half] = plain_ref[now, :half] - sign * plain_ref[prior, half:]
        full_ref[now, half:] = plain_ref[now, half:] + sign * plain_ref[prior, :half]


def pair_sums(out_ref, one_ref, lag_ref, chans, panels, forward):
    half = out_ref.shape[1] // 2
    group = 4
    for lane in range(0, half, 128):

        def step(row, carry):
            start = pl.multiple_of(row * 8, 8)

            def load(ref, panel):
                rows = pl.ds(panel * chans + start, 8)
                return ref[rows, lane : lane + 128], ref[rows, half + lane : half + lane + 128]

            for first in range(0, panels, group):
                sums = [None] * group
                ones = {}
                lags = range(first + group) if forward else range(panels - first)
                for lag in lags:
                    lag_re, lag_im = load(lag_ref, lag)
                    for at in range(group):
                        other = first + at - lag if forward else first + at + lag
                        if not 0 <= other < panels:
                            continue
                        if other not in ones:
                            ones[other] = load(one_ref, other)
                        one_re, one_im = ones[other]
                        if forward:
                            re = one_re * lag_re - one_im * lag_im
                            im = one_re * lag_im + one_im * lag_re
                        else:
                            re = one_re * lag_re + one_im * lag_im
                            im = one_im * lag_re - one_re * lag_im
                        held = sums[at]
                        sums[at] = (re, im) if held is None else (held[0] + re, held[1] + im)
                for at in range(group):
                    rows = pl.ds((first + at) * chans + start, 8)
                    out_ref[rows, lane : lane + 128] = sums[at][0]
                    out_ref[rows, half + lane : half + lane + 128] = sums[at][1]
            return carry

        lax.fori_loop(0, chans // 8, step, 0)


def by_rows(ref, at, chans):
    part = ref[:, at * chans : (at + 1) * chans, :]
    return part.reshape(part.shape[0] * chans, part.shape[2])


def send_kernel(
    panels, signal_in, gate_in, grad_in, filter_in, out_ref, signal_ref, gate_ref, grad_ref, filter_ref, sems
):
    chans = out_ref.shape[1] // 3
    copies = []
    for at, (source, target) in enumerate(
        ((gate_in, gate_ref), (grad_in, grad_ref), (filter_in, filter_ref), (signal_in, signal_ref))
    ):
        copies.append(pltpu.make_async_copy(source, target, sems.at[at]))
        copies[-1].start()

    def put(at, panel):
        parts = panel.T.reshape(panels, chans, panel.shape[0])
        out_ref[:, at * chans : (at + 1) * chans, :] = parts

    copies[0].wait()
    copies[1].wait()
    gated = gate_ref[...].astype(jnp.float32) * grad_ref[...].astype(jnp.float32)
    put(0, gated.astype(jnp.bfloat16))
    copies[2].wait()
    put(1, filter_ref[...])
    copies[3].wait()
    put(2, signal_ref[...])


def signal_grad_kernel(
    panels, parts_ref, high_ref, low_ref, grad_ref, gated_spec, filter_full, plain, sums
):
    chans = parts_ref.shape[1] // 3
    gated_spec[...] = spectra(by_rows(parts_ref, 0, chans), high_ref, low_ref)
    plain[...] = spectra(by_rows(parts_ref, 1, chans), high_ref, low_ref)
    widen(plain, filter_full, chans, panels)
    pair_sums(sums, gated_spec, filter_full, chans, panels, False)
    grad_ref[...] = inverse(sums[...], high_ref, low_ref).astype(grad_ref.dtype)


def rest_kernel(
    panels, parts_ref, high_ref, low_ref, out_ref, gated_spec, signal_spec, filter_spec, full, sums
):
    chans = parts_ref.shape[1] // 3

    def put(at):
        grad = inverse(sums[...], high_ref, low_ref).astype(out_ref.dtype)
        out_ref[:, at * chans : (at + 1) * chans, :] = grad.reshape(panels, chans, grad.shape[1])

    for at, spec in enumerate((gated_spec, filter_spec, signal_spec)):
        spec[...] = spectra(by_rows(parts_ref, at, chans), high_ref, low_ref)
    widen(signal_spec, full, chans, panels)
    pair_sums(sums, filter_spec, full, chans, panels, True)
    put(0)
    pair_sums(sums, gated_spec, full, chans, panels, False)
    put(1)


def weight_kernel(starts_ref, weight_ref, *refs):
    count = (len(refs) - 1) // 2
    outs, helds, sems = refs[:count], refs[count:-1], refs[-1]
    loads, stores = [], []
    for at in range(count):
        rows = outs[at].shape[0]
        start = pl.multiple_of(starts_ref[at], 256)
        loads.append(
            pltpu.make_async_copy(weight_ref.at[pl.ds(start, rows)], helds[at], sems.at[0, at])
        )
        stores.append(pltpu.make_async_copy(helds[at], outs[at], sems.at[1, at]))
        loads[at].start()
    for at in range(count):
        loads[at].wait()
        stores[at].start()
    for store in stores:
        store.wait()


def finish_kernel(panels, parts_ref, grad_ref, token_ref, gate_out, filter_out):
    chans = parts_ref.shape[1] // 2
    conv = by_rows(parts_ref, 0, chans).T.astype(jnp.float32)
    gate_out[...] = (grad_ref[...].astype(jnp.float32) * conv).astype(gate_out.dtype)
    filter_out[...] = by_rows(parts_ref, 1, chans).T.astype(jnp.float32)


def project_kernel(panels, *refs):
    count = (len(refs) - 3) // 3
    total_ref, blocks, weights = refs[0], refs[1 : 1 + count], refs[1 + count : 1 + 2 * count]
    out_ref, held, sems = refs[1 + 2 * count], refs[2 + 2 * count : -1], refs[-1]
    copies = [pltpu.make_async_copy(weights[at], held[at], sems.at[at]) for at in range(count)]
    for copy in copies:
        copy.start()
    total = total_ref[...]
    for at in range(count):
        block = blocks[at][...].T
        copies[at].wait()
        total = total + lax.dot_general(
            block, held[at][...], (((1,), (1,)), ((), ())), preferred_element_type=jnp.float32
        )
    out_ref[...] = total.astype(out_ref.dtype)


def last_kernel(panels, total_ref, block_ref, weight_ref, out_ref, held, done, sems):
    count = sems.shape[1]
    size = out_ref.shape[1] // count
    columns = [pl.ds(at * size, size) for at in range(count)]
    loads = [
        pltpu.make_async_copy(weight_ref.at[part], held.at[part], sems.at[0, at])
        for at, part in enumerate(columns)
    ]
    stores = [
        pltpu.make_async_copy(done.at[:, part], out_ref.at[:, part], sems.at[1, at])
        for at, part in enumerate(columns)
    ]
    for load in loads:
        load.start()
    block = block_ref[...].T
    for at, part in enumerate(columns):
        loads[at].wait()
        total = total_ref[:, part] + lax.dot_general(
            block, held[part, :], (((1,), (1,)), ((), ())), preferred_element_type=jnp.float32
        )
        done[:, part] = total.astype(done.dtype)
        stores[at].start()
    for store in stores:
        store.wait()


def call(kernel, panels, outs, scratch, *operands, space=pltpu.VMEM, streamed=0, cost=None, out_space=pltpu.VMEM):
    return pl.pallas_call(
        lambda *refs: kernel(panels, *refs),
        out_shape=outs,
        in_specs=[pl.BlockSpec(memory_space=space)] * (len(operands) - streamed)
        + [pl.BlockSpec(memory_space=pltpu.HBM)] * streamed,
        out_specs=[pl.BlockSpec(memory_space=out_space)] * len(outs),
        scratch_shapes=scratch,
        cost_estimate=cost,
        compiler_params=pltpu.CompilerParams(vmem_limit_bytes=16 * 1024 * 1024),
    )(*operands)


def shifted(x, axis, by):
    length = lax.axis_size(axis)
    return lax.ppermute(x, axis, [(i, (i + by) % length) for i in range(length)])


def on_device(signal, gate_value, grad_out, long_filter, weight):
    panel_len, width = signal.shape[1:]
    panels = lax.axis_size("seq")
    groups = lax.axis_size("chan")
    chans = width // panels
    rows = panels * chans
    high, low = make_tables(panel_len)
    high, low = jnp.asarray(high), jnp.asarray(low)

    def swapped(parts):
        return lax.all_to_all(parts, "seq", 0, 0, tiled=True)

    def shape(*dims, dtype=jnp.bfloat16):
        return jax.ShapeDtypeStruct(dims, dtype)

    (sent,) = call(
        send_kernel,
        panels,
        (pltpu.HBM((panels, 3 * chans, panel_len), jnp.bfloat16),),
        [pltpu.VMEM((panel_len, width), jnp.bfloat16)] * 4 + [pltpu.SemaphoreType.DMA((4,))],
        *(
            pltpu.with_memory_space_constraint(panel[0], pltpu.HBM)
            for panel in (signal, gate_value, grad_out, long_filter)
        ),
        space=pltpu.HBM,
    )
    parts = swapped(sent)

    my_group = lax.axis_index("chan")
    outputs = weight.shape[1] // groups
    starts = [outputs * lax.rem(my_group + by, groups) for by in (1, 3, 2)]
    weight_parts = pl.pallas_call(
        weight_kernel,
        out_shape=[pltpu.HBM((outputs, width), jnp.bfloat16)] * 3,
        in_specs=[
            pl.BlockSpec(memory_space=pltpu.SMEM),
            pl.BlockSpec(memory_space=pltpu.HBM),
        ],
        out_specs=[pl.BlockSpec(memory_space=pltpu.HBM)] * 3,
        scratch_shapes=[pltpu.VMEM((outputs, width), jnp.bfloat16)] * 3
        + [pltpu.SemaphoreType.DMA((2, 3))],
        compiler_params=pltpu.CompilerParams(vmem_limit_bytes=16 * 1024 * 1024),
    )(jnp.stack(starts), pltpu.with_memory_space_constraint(weight[0], pltpu.HBM))
    weights = [shifted(part, "chan", by) for part, by in zip(weight_parts, (1, 3, 2))]

    held = pltpu.VMEM((rows, 2 * panel_len), jnp.float32)
    (signal_grad,) = call(
        signal_grad_kernel,
        panels,
        (pltpu.HBM((rows, panel_len), jnp.bfloat16),),
        [held] * 4,
        parts,
        high,
        low,
    )
    signal_grad = swapped(signal_grad.reshape(panels, chans, panel_len)).reshape(width, panel_len)
    (rest,) = call(
        rest_kernel,
        panels,
        (pltpu.HBM((panels, 2 * chans, panel_len), jnp.bfloat16),),
        [held] * 5,
        parts,
        high,
        low,
    )
    signal_grad, rest = lax.optimization_barrier((signal_grad, rest))
    received = shifted(signal_grad, "pipe", -1)
    token = lax.ppermute(signal_grad[:16, :128], "seq", [(i, i ^ 1) for i in range(panels)])
    rest, token = lax.optimization_barrier((rest, token))
    rest = swapped(rest)
    received, weights = lax.optimization_barrier((received, weights))

    def project(block, block_weight):
        return lax.dot_general(
            block, block_weight, (((0,), (1,)), ((), ())), preferred_element_type=jnp.float32
        )

    gate_grad, filter_grad = call(
        finish_kernel,
        panels,
        (shape(panel_len, width), shape(panel_len, width, dtype=jnp.float32)),
        [],
        rest,
        grad_out[0],
        token,
    )
    total = project(received, lax.dynamic_slice_in_dim(weight[0], my_group * outputs, outputs, 0))
    blocks = [shifted(received, "chan", by) for by in (1, 3, 2)]

    def add_blocks(total, which, dtype):
        count = len(which)
        (added,) = call(
            project_kernel,
            panels,
            (shape(panel_len, outputs, dtype=dtype),),
            [pltpu.VMEM((outputs, width), jnp.bfloat16)] * count
            + [pltpu.SemaphoreType.DMA((count,))],
            total,
            *(blocks[at] for at in which),
            *(pltpu.with_memory_space_constraint(weights[at], pltpu.HBM) for at in which),
            streamed=count,
            cost=pl.CostEstimate(
                flops=HINT_SCALE * 2 * count * panel_len * width * outputs,
                transcendentals=0,
                bytes_accessed=HINT_SCALE * 2 * count * outputs * width,
            ),
        )
        return added

    blocks[:2], total = lax.optimization_barrier((blocks[:2], total))
    total = add_blocks(total, (0, 1), jnp.float32)
    blocks[2], total, gate_grad, filter_grad = lax.optimization_barrier(
        (blocks[2], total, gate_grad, filter_grad)
    )
    (input_grad,) = call(
        last_kernel,
        panels,
        (pltpu.HBM((panel_len, outputs), jnp.bfloat16),),
        [
            pltpu.VMEM((outputs, width), jnp.bfloat16),
            pltpu.VMEM((panel_len, outputs), jnp.bfloat16),
            pltpu.SemaphoreType.DMA((2, 4)),
        ],
        total,
        blocks[2],
        pltpu.with_memory_space_constraint(weights[2], pltpu.HBM),
        streamed=1,
        out_space=pltpu.HBM,
        cost=pl.CostEstimate(
            flops=HINT_SCALE * 2 * panel_len * width * outputs,
            transcendentals=0,
            bytes_accessed=HINT_SCALE * 2 * outputs * width,
        ),
    )
    return gate_grad[None], filter_grad[None], input_grad[None]


def solution(mesh):
    return jax.shard_map(
        on_device,
        mesh=mesh,
        in_specs=(
            P("pipe", "seq", "chan"),
            P("pipe", "seq", "chan"),
            P("pipe", "seq", "chan"),
            P("pipe", "seq", "chan"),
            P("pipe", None, "chan"),
        ),
        out_specs=(P("pipe", "seq", "chan"), P("pipe", "seq", "chan"), P("pipe", "seq", "chan")),
        check_vma=False,
    )
```

```python
import jax
import jax.numpy as jnp
import ml_dtypes
import numpy as np
from jax import lax
from jax.experimental import pallas as pl
from jax.experimental.pallas import tpu as pltpu
from jax.sharding import PartitionSpec as P


HINT_SCALE = 8


def make_tables(panel_len):
    position = np.arange(panel_len)[:, None]
    odd = 2 * np.arange(panel_len)[None, :] + 1
    angles = (position * odd % (4 * panel_len)) * (np.pi / (2 * panel_len))
    table = np.concatenate([np.cos(angles), -np.sin(angles)], axis=1)
    high = table.astype(np.float32).astype(ml_dtypes.bfloat16)
    low = (table - high.astype(np.float64)).astype(np.float32).astype(ml_dtypes.bfloat16)
    return high, low


def dot(left, right):
    return jnp.dot(left, right, preferred_element_type=jnp.float32)


def spectra(rows, high_ref, low_ref):
    return dot(rows, high_ref[...]) + dot(rows, low_ref[...])


def inverse(spec, high_ref, low_ref):
    panel_len = high_ref.shape[0]
    top = spec.astype(jnp.bfloat16)
    rest = (spec - top.astype(jnp.float32)).astype(jnp.bfloat16)
    dims = (((1,), (1,)), ((), ()))

    def back(left, right):
        return lax.dot_general(left, right, dims, preferred_element_type=jnp.float32)

    high = high_ref[...]
    return (back(top, high) + (back(rest, high) + back(top, low_ref[...]))) * (1.0 / panel_len)


def widen(plain_ref, full_ref, chans, panels):
    half = plain_ref.shape[1] // 2
    sign = 1.0 - 2.0 * (lax.broadcasted_iota(jnp.int32, (chans, half), 1) % 2).astype(jnp.float32)
    full_ref[pl.ds(0, chans), :] = plain_ref[pl.ds(0, chans), :]
    for panel in range(1, panels):
        now, prior = pl.ds(panel * chans, chans), pl.ds((panel - 1) * chans, chans)
        full_ref[now, :half] = plain_ref[now, :half] - sign * plain_ref[prior, half:]
        full_ref[now, half:] = plain_ref[now, half:] + sign * plain_ref[prior, :half]


def pair_sums(out_ref, one_ref, lag_ref, chans, panels, forward):
    half = out_ref.shape[1] // 2
    group = 4
    for lane in range(0, half, 128):

        def step(row, carry):
            start = pl.multiple_of(row * 8, 8)

            def load(ref, panel):
                rows = pl.ds(panel * chans + start, 8)
                return ref[rows, lane : lane + 128], ref[rows, half + lane : half + lane + 128]

            for first in range(0, panels, group):
                sums = [None] * group
                ones = {}
                lags = range(first + group) if forward else range(panels - first)
                for lag in lags:
                    lag_re, lag_im = load(lag_ref, lag)
                    for at in range(group):
                        other = first + at - lag if forward else first + at + lag
                        if not 0 <= other < panels:
                            continue
                        if other not in ones:
                            ones[other] = load(one_ref, other)
                        one_re, one_im = ones[other]
                        if forward:
                            re = one_re * lag_re - one_im * lag_im
                            im = one_re * lag_im + one_im * lag_re
                        else:
                            re = one_re * lag_re + one_im * lag_im
                            im = one_im * lag_re - one_re * lag_im
                        held = sums[at]
                        sums[at] = (re, im) if held is None else (held[0] + re, held[1] + im)
                for at in range(group):
                    rows = pl.ds((first + at) * chans + start, 8)
                    out_ref[rows, lane : lane + 128] = sums[at][0]
                    out_ref[rows, half + lane : half + lane + 128] = sums[at][1]
            return carry

        lax.fori_loop(0, chans // 8, step, 0)


def by_rows(ref, at, chans):
    part = ref[:, at * chans : (at + 1) * chans, :]
    return part.reshape(part.shape[0] * chans, part.shape[2])


def send_kernel(
    panels, signal_in, gate_in, grad_in, filter_in, out_ref, signal_ref, gate_ref, grad_ref, filter_ref, sems
):
    chans = out_ref.shape[1] // 3
    copies = []
    for at, (source, target) in enumerate(
        ((gate_in, gate_ref), (grad_in, grad_ref), (filter_in, filter_ref), (signal_in, signal_ref))
    ):
        copies.append(pltpu.make_async_copy(source, target, sems.at[at]))
        copies[-1].start()

    def put(at, panel):
        parts = panel.T.reshape(panels, chans, panel.shape[0])
        out_ref[:, at * chans : (at + 1) * chans, :] = parts

    copies[0].wait()
    copies[1].wait()
    gated = gate_ref[...].astype(jnp.float32) * grad_ref[...].astype(jnp.float32)
    put(0, gated.astype(jnp.bfloat16))
    copies[2].wait()
    put(1, filter_ref[...])
    copies[3].wait()
    put(2, signal_ref[...])


def signal_grad_kernel(
    panels, parts_ref, high_ref, low_ref, grad_ref, gated_spec, filter_full, plain, sums
):
    chans = parts_ref.shape[1] // 3
    gated_spec[...] = spectra(by_rows(parts_ref, 0, chans), high_ref, low_ref)
    plain[...] = spectra(by_rows(parts_ref, 1, chans), high_ref, low_ref)
    widen(plain, filter_full, chans, panels)
    pair_sums(sums, gated_spec, filter_full, chans, panels, False)
    grad_ref[...] = inverse(sums[...], high_ref, low_ref).astype(grad_ref.dtype)


def rest_kernel(
    panels, parts_ref, high_ref, low_ref, out_ref, gated_spec, signal_spec, filter_spec, full, sums
):
    chans = parts_ref.shape[1] // 3

    def put(at):
        grad = inverse(sums[...], high_ref, low_ref).astype(out_ref.dtype)
        out_ref[:, at * chans : (at + 1) * chans, :] = grad.reshape(panels, chans, grad.shape[1])

    for at, spec in enumerate((gated_spec, filter_spec, signal_spec)):
        spec[...] = spectra(by_rows(parts_ref, at, chans), high_ref, low_ref)
    widen(signal_spec, full, chans, panels)
    pair_sums(sums, filter_spec, full, chans, panels, True)
    put(0)
    pair_sums(sums, gated_spec, full, chans, panels, False)
    put(1)


def weight_kernel(starts_ref, weight_ref, *refs):
    count = (len(refs) - 1) // 2
    outs, helds, sems = refs[:count], refs[count:-1], refs[-1]
    loads, stores = [], []
    for at in range(count):
        rows = outs[at].shape[0]
        start = pl.multiple_of(starts_ref[at], 256)
        loads.append(
            pltpu.make_async_copy(weight_ref.at[pl.ds(start, rows)], helds[at], sems.at[0, at])
        )
        stores.append(pltpu.make_async_copy(helds[at], outs[at], sems.at[1, at]))
        loads[at].start()
    for at in range(count):
        loads[at].wait()
        stores[at].start()
    for store in stores:
        store.wait()


def finish_kernel(panels, parts_ref, grad_ref, token_ref, gate_out, filter_out):
    chans = parts_ref.shape[1] // 2
    conv = by_rows(parts_ref, 0, chans).T.astype(jnp.float32)
    gate_out[...] = (grad_ref[...].astype(jnp.float32) * conv).astype(gate_out.dtype)
    filter_out[...] = by_rows(parts_ref, 1, chans).T.astype(jnp.float32)


def project_kernel(panels, *refs):
    count = (len(refs) - 3) // 3
    total_ref, blocks, weights = refs[0], refs[1 : 1 + count], refs[1 + count : 1 + 2 * count]
    out_ref, held, sems = refs[1 + 2 * count], refs[2 + 2 * count : -1], refs[-1]
    copies = [pltpu.make_async_copy(weights[at], held[at], sems.at[at]) for at in range(count)]
    for copy in copies:
        copy.start()
    total = total_ref[...]
    for at in range(count):
        block = blocks[at][...].T
        copies[at].wait()
        total = total + lax.dot_general(
            block, held[at][...], (((1,), (1,)), ((), ())), preferred_element_type=jnp.float32
        )
    out_ref[...] = total.astype(out_ref.dtype)


def call(kernel, panels, outs, scratch, *operands, space=pltpu.VMEM, streamed=0, cost=None):
    return pl.pallas_call(
        lambda *refs: kernel(panels, *refs),
        out_shape=outs,
        in_specs=[pl.BlockSpec(memory_space=space)] * (len(operands) - streamed)
        + [pl.BlockSpec(memory_space=pltpu.HBM)] * streamed,
        out_specs=[pl.BlockSpec(memory_space=pltpu.VMEM)] * len(outs),
        scratch_shapes=scratch,
        cost_estimate=cost,
        compiler_params=pltpu.CompilerParams(vmem_limit_bytes=16 * 1024 * 1024),
    )(*operands)


def shifted(x, axis, by):
    length = lax.axis_size(axis)
    return lax.ppermute(x, axis, [(i, (i + by) % length) for i in range(length)])


def on_device(signal, gate_value, grad_out, long_filter, weight):
    panel_len, width = signal.shape[1:]
    panels = lax.axis_size("seq")
    groups = lax.axis_size("chan")
    chans = width // panels
    rows = panels * chans
    high, low = make_tables(panel_len)
    high, low = jnp.asarray(high), jnp.asarray(low)

    def swapped(parts):
        return lax.all_to_all(parts, "seq", 0, 0, tiled=True)

    def shape(*dims, dtype=jnp.bfloat16):
        return jax.ShapeDtypeStruct(dims, dtype)

    (sent,) = call(
        send_kernel,
        panels,
        (pltpu.HBM((panels, 3 * chans, panel_len), jnp.bfloat16),),
        [pltpu.VMEM((panel_len, width), jnp.bfloat16)] * 4 + [pltpu.SemaphoreType.DMA((4,))],
        *(
            pltpu.with_memory_space_constraint(panel[0], pltpu.HBM)
            for panel in (signal, gate_value, grad_out, long_filter)
        ),
        space=pltpu.HBM,
    )
    parts = swapped(sent)

    my_group = lax.axis_index("chan")
    outputs = weight.shape[1] // groups
    starts = [outputs * lax.rem(my_group + by, groups) for by in (1, 3, 2)]
    weight_parts = pl.pallas_call(
        weight_kernel,
        out_shape=[pltpu.HBM((outputs, width), jnp.bfloat16)] * 3,
        in_specs=[
            pl.BlockSpec(memory_space=pltpu.SMEM),
            pl.BlockSpec(memory_space=pltpu.HBM),
        ],
        out_specs=[pl.BlockSpec(memory_space=pltpu.HBM)] * 3,
        scratch_shapes=[pltpu.VMEM((outputs, width), jnp.bfloat16)] * 3
        + [pltpu.SemaphoreType.DMA((2, 3))],
        compiler_params=pltpu.CompilerParams(vmem_limit_bytes=16 * 1024 * 1024),
    )(jnp.stack(starts), pltpu.with_memory_space_constraint(weight[0], pltpu.HBM))
    weights = [shifted(part, "chan", by) for part, by in zip(weight_parts, (1, 3, 2))]

    held = pltpu.VMEM((rows, 2 * panel_len), jnp.float32)
    (signal_grad,) = call(
        signal_grad_kernel,
        panels,
        (pltpu.HBM((rows, panel_len), jnp.bfloat16),),
        [held] * 4,
        parts,
        high,
        low,
    )
    signal_grad = swapped(signal_grad.reshape(panels, chans, panel_len)).reshape(width, panel_len)
    (rest,) = call(
        rest_kernel,
        panels,
        (pltpu.HBM((panels, 2 * chans, panel_len), jnp.bfloat16),),
        [held] * 5,
        parts,
        high,
        low,
    )
    signal_grad, rest = lax.optimization_barrier((signal_grad, rest))
    received = shifted(signal_grad, "pipe", -1)
    token = lax.ppermute(signal_grad[:16, :128], "seq", [(i, i ^ 1) for i in range(panels)])
    rest, token = lax.optimization_barrier((rest, token))
    rest = swapped(rest)
    received, weights = lax.optimization_barrier((received, weights))

    def project(block, block_weight):
        return lax.dot_general(
            block, block_weight, (((0,), (1,)), ((), ())), preferred_element_type=jnp.float32
        )

    total = project(received, lax.dynamic_slice_in_dim(weight[0], my_group * outputs, outputs, 0))
    blocks = [shifted(received, "chan", by) for by in (1, 3, 2)]

    def add_blocks(total, which, dtype):
        count = len(which)
        (added,) = call(
            project_kernel,
            panels,
            (shape(panel_len, outputs, dtype=dtype),),
            [pltpu.VMEM((outputs, width), jnp.bfloat16)] * count
            + [pltpu.SemaphoreType.DMA((count,))],
            total,
            *(blocks[at] for at in which),
            *(pltpu.with_memory_space_constraint(weights[at], pltpu.HBM) for at in which),
            streamed=count,
            cost=pl.CostEstimate(
                flops=HINT_SCALE * 2 * count * panel_len * width * outputs,
                transcendentals=0,
                bytes_accessed=HINT_SCALE * 2 * count * outputs * width,
            ),
        )
        return added

    input_grad = add_blocks(total, (0, 1, 2), jnp.bfloat16)
    rest, input_grad = lax.optimization_barrier((rest, input_grad))
    gate_grad, filter_grad = call(
        finish_kernel,
        panels,
        (shape(panel_len, width), shape(panel_len, width, dtype=jnp.float32)),
        [],
        rest,
        grad_out[0],
        token,
    )
    return gate_grad[None], filter_grad[None], input_grad[None]


def solution(mesh):
    return jax.shard_map(
        on_device,
        mesh=mesh,
        in_specs=(
            P("pipe", "seq", "chan"),
            P("pipe", "seq", "chan"),
            P("pipe", "seq", "chan"),
            P("pipe", "seq", "chan"),
            P("pipe", None, "chan"),
        ),
        out_specs=(P("pipe", "seq", "chan"), P("pipe", "seq", "chan"), P("pipe", "seq", "chan")),
        check_vma=False,
    )
```
